32 devices in a mesh: parts: 2 (over x), rows: 16 (over z, y, core).
Axes of the slice: x: 2, y: 2, z: 4, core: 2. Of those that a mesh axis runs over, the one named last changes fastest.
Arguments:
- estimate: float32 [256, 2048], P(('parts', 'rows')), parts along dimension 0, may hold values from -6 to 6
- observed: float32 [256, 2048], P('parts', 'rows'), parts along dimension 0, may hold values from -6 to 6
- cotangent: float32 [256, 2048], P(('parts', 'rows')), parts along dimension 0
- zone_map: int32 [2, 16], P('parts'), parts along dimension 0, may hold values from 0 to 7
- bank_pick: int32 [2, 8], replicated, may hold values from 0 to 7
- psf_bank: float32 [8, 25], replicated, may hold values from 0.01 to 1
- w_first: bfloat16 [32, 1, 3, 3], replicated, may hold values from -2 to 2
- w_mid: bfloat16 [32, 32, 3, 3], replicated, may hold values from -0.375 to 0.375
- w_last: bfloat16 [1, 32, 3, 3], replicated, may hold values from -0.375 to 0.375
Outputs:
- denoised: float32 [256, 2048], P(('parts', 'rows')), parts along dimension 0
- grad_estimate: float32 [256, 2048], P(('parts', 'rows')), parts along dimension 0
- grad_first: float32 [64, 1, 3, 3], P('parts'), parts along dimension 0
- grad_mid: float32 [64, 32, 3, 3], P('parts'), parts along dimension 0
- grad_last: float32 [2, 32, 3, 3], P('parts'), parts along dimension 0
The draws below stay inside these ranges and needn't reach their ends.
There are 2 independent parts, one for each index of `parts`. The reference program is written for one: setup_inputs(seed, part) draws one part's arguments, and reference() takes and returns one part's arrays. A program takes and returns all parts, laid end to end along the dimension named above; an argument that names none is the same for every part. Nothing has to cross between parts.
All inputs are finite; a program needn't handle non-finite values.
Results may differ from the reference program's by a relative error of at most 0.0071.
Values may be sent and summed in bfloat16 or wider, within the bound.
A program may use at most 256 MiB of HBM per device.

```python
import math
import jax
import jax.numpy as jnp
from jax import lax

BLK = 128
RAD = 12
ZONES = 8
BANK = 8
CH = 32
TAPS = 25
HEIGHT = 128
WIDTH = 2048


def draw_cotangent(key, part):
    position = jnp.arange(HEIGHT, dtype=jnp.float32) / max(HEIGHT - 1, 1)
    growth = jnp.exp(math.log(3.0) * position)
    sample = jax.random.normal(key, (HEIGHT, WIDTH), jnp.float32)
    result = sample * growth[:, None] / 1.7
    return result.astype(jnp.float32)


def place_ends(drawn, own_key, low, top_value):
    shape = drawn.shape
    index_at = [jax.random.randint(jax.random.fold_in(own_key, axis), (), 0, shape[axis]) for axis in range(len(shape))]
    drawn = drawn.at[tuple(index_at)].set(low)
    longest = shape.index(max(shape))
    index_at[longest] = (index_at[longest] + 1) % shape[longest]
    return drawn.at[tuple(index_at)].set(top_value)


def levels(rng, shape, pieces, least, top_value):
    loudness = 1.0
    for dim, shards_of in pieces:
        steps = jax.random.uniform(jax.random.fold_in(jax.random.fold_in(rng, 6), dim), (shards_of,), jnp.float32, least / len(pieces), top_value / len(pieces))
        loudness = loudness * jnp.repeat(jnp.exp(steps), shape[dim] // shards_of).reshape((-1,) + (1,) * (len(shape) - 1 - dim))
    return loudness


def bell_draw(stream_key, extent, scale, most, split=(), kind=jnp.bfloat16):
    values = scale * jax.random.normal(stream_key, extent, jnp.float32)
    if split:
        values = values * levels(stream_key, extent, split, -0.22, 0.18)
    return jnp.clip(values, -most, most).astype(kind)


def setup_inputs(seed: int = 0, part: int = 0) -> dict:
    arg_keys = jax.random.split(jax.random.key(seed), 10)
    part_keys = jax.random.split(jax.random.fold_in(arg_keys[9], part), 10)
    return {
        "estimate": bell_draw(part_keys[0], (HEIGHT, WIDTH), 1.0, 6.0, ((0, 16),), jnp.float32),
        "observed": bell_draw(part_keys[1], (HEIGHT, WIDTH), 1.0, 6.0, ((1, 16),), jnp.float32),
        "cotangent": draw_cotangent(jax.random.fold_in(jax.random.fold_in(arg_keys[9], part), 71), part),
        "zone_map": place_ends(jax.random.randint(part_keys[3], (HEIGHT // BLK, WIDTH // BLK), 0, ZONES), jax.random.fold_in(part_keys[3], 1), 0, ZONES - 1).astype(jnp.int32),
        "bank_pick": place_ends(jax.random.randint(arg_keys[4], (2, ZONES), 0, BANK), jax.random.fold_in(arg_keys[4], 1), 0, BANK - 1).astype(jnp.int32),
        "psf_bank": jnp.clip(jnp.exp(jax.random.uniform(arg_keys[5], (BANK, TAPS), jnp.float32, math.log(0.01), math.log(1.0))), 0.01, 1.0),
        "w_first": bell_draw(arg_keys[6], (CH, 1, 3, 3), 9 ** -0.5, 2.0),
        "w_mid": bell_draw(arg_keys[7], (CH, CH, 3, 3), (9 * CH) ** -0.5, 0.375),
        "w_last": bell_draw(arg_keys[8], (1, CH, 3, 3), (9 * CH) ** -0.5, 0.375),
    }


STEP_SIZE = 2.0
GRAD_FACTOR = 8.0

def silu_slope(values):
    sigmoid = jax.nn.sigmoid(values)
    return sigmoid * (1.0 + values * (1.0 - sigmoid))

def flipped(weight):
    return jnp.transpose(jnp.flip(weight, (2, 3)), (1, 0, 2, 3))

def conv_rows(padded, weight):
    result = lax.conv_general_dilated(padded[None], weight, (1, 1), ((0, 0), (1, 1)), dimension_numbers=('NCHW', 'OIHW', 'NCHW'), preferred_element_type=jnp.float32)
    return result[0]

def weight_grad(padded, errors):
    framed = jnp.pad(padded, ((0, 0), (0, 0), (1, 1)))
    result = lax.conv_general_dilated(framed[None], errors[None], (1, 1), 'VALID', dimension_numbers=('CNHW', 'IOHW', 'NCHW'), preferred_element_type=jnp.float32)
    return jnp.transpose(result, (1, 0, 2, 3))

def blur_full(values, coef_at, along, adjoint):
    length = values.shape[along]
    widths = [(0, 0), (0, 0)]
    widths[along] = (RAD, RAD)
    summed = jnp.zeros_like(values)
    padded = jnp.pad(values, widths)
    for offset in range(2 * RAD + 1):
        factor = coef_at(offset)
        if adjoint:
            spread = jnp.pad(factor * values, widths)
            summed = summed + lax.slice_in_dim(spread, 2 * RAD - offset, 2 * RAD - offset + length, axis=along)
        else:
            summed = summed + factor * lax.slice_in_dim(padded, offset, offset + length, axis=along)
    return summed

def reference(estimate, observed, cotangent, zone_map, bank_pick, psf_bank, w_first, w_mid, w_last):
    norm_bank = psf_bank / lax.optimization_barrier(jnp.sum(psf_bank, axis=1, keepdims=True))
    kernels = norm_bank[bank_pick]
    zone_full = jnp.repeat(jnp.repeat(zone_map, BLK, axis=0), BLK, axis=1)

    def row_coef(offset):
        return kernels[0, :, offset][zone_full]

    def col_coef(offset):
        return kernels[1, :, offset][zone_full]

    def gradient_of(values, target):
        blurred = blur_full(values, row_coef, 1, False)
        blurred = blur_full(blurred, col_coef, 0, False)
        if target is not None:
            blurred = blurred - target
        spread = blur_full(blurred, col_coef, 0, True)
        return blur_full(spread, row_coef, 1, True)
    data_step = estimate - STEP_SIZE * gradient_of(estimate, observed)
    block_rows = BLK
    block_count = HEIGHT // block_rows
    step_pad = jnp.pad(data_step, ((4, 4), (0, 0)))
    cot_pad = jnp.pad(cotangent, ((3, 3), (0, 0)))

    def one_block(carry, block_index):
        first_row = block_index * block_rows
        step_ext = lax.dynamic_slice_in_dim(step_pad, first_row, block_rows + 8, 0)
        cot_ext = lax.dynamic_slice_in_dim(cot_pad, first_row, block_rows + 6, 0)

        def inside(offset, count_rows):
            row_ids = first_row + offset + jnp.arange(count_rows, dtype=jnp.int32)
            return ((row_ids >= 0) & (row_ids < HEIGHT)).astype(jnp.bfloat16)[None, :, None]
        first_in = step_ext.astype(jnp.bfloat16)[None]
        pre_first = conv_rows(first_in, w_first)
        act_first = jax.nn.silu(pre_first).astype(jnp.bfloat16) * inside(-3, block_rows + 6)
        pre_mid = conv_rows(act_first, w_mid)
        act_mid = jax.nn.silu(pre_mid).astype(jnp.bfloat16) * inside(-2, block_rows + 4)
        denoised = step_ext[4:4 + block_rows] + conv_rows(act_mid[:, 1:block_rows + 3], w_last)[0]
        cot_in = cot_ext.astype(jnp.bfloat16)[None]
        back_mid = (conv_rows(cot_in, flipped(w_last)) * silu_slope(pre_mid)).astype(jnp.bfloat16) * inside(-2, block_rows + 4)
        back_first = (conv_rows(back_mid, flipped(w_mid)) * silu_slope(pre_first[:, 2:block_rows + 4])).astype(jnp.bfloat16) * inside(-1, block_rows + 2)
        grad_data = cot_ext[3:3 + block_rows] + conv_rows(back_first, flipped(w_first))[0]
        grad_last = weight_grad(act_mid[:, 1:block_rows + 3], cot_in[:, 3:3 + block_rows])
        grad_mid = weight_grad(act_first[:, 2:block_rows + 4], back_mid[:, 2:2 + block_rows])
        grad_first = weight_grad(first_in[:, 3:block_rows + 5], back_first[:, 1:1 + block_rows])
        carry = (carry[0] + grad_first, carry[1] + grad_mid, carry[2] + grad_last)
        return (carry, (denoised, grad_data))
    start_sums = (jnp.zeros(w_first.shape, jnp.float32), jnp.zeros(w_mid.shape, jnp.float32), jnp.zeros(w_last.shape, jnp.float32))
    sums, outputs = lax.scan(one_block, start_sums, jnp.arange(block_count, dtype=jnp.int32))
    denoised = outputs[0].reshape(HEIGHT, WIDTH)
    grad_data = outputs[1].reshape(HEIGHT, WIDTH)
    grad_scale = GRAD_FACTOR / math.sqrt(HEIGHT * WIDTH)
    grad_estimate = grad_data - STEP_SIZE * gradient_of(grad_data, None)
    return (denoised, grad_estimate, sums[0] * grad_scale, sums[1] * grad_scale, sums[2] * grad_scale)
```

```python
import functools
import math

import jax
import jax.numpy as jnp
import numpy as np
from jax import lax
from jax.experimental import pallas as pl
from jax.experimental.pallas import tpu as pltpu
from jax.sharding import PartitionSpec as P

BLK = 128
RAD = 12
TAPS = 2 * RAD + 1
CH = 32
BAND = 8
STEP_SIZE = 2.0
GRAD_FACTOR = 8.0
MESH = pl.DeviceIdType.MESH
F32 = jnp.float32
BF16 = jnp.bfloat16

EXT_ROWS = list(range(8)) + [-4, -3, -2, -1, 8, 9, 10, 11]


def band_select(out_rows, in_rows, sign):
    table = np.zeros((len(out_rows), len(in_rows), 3), np.float32)
    for i, r in enumerate(out_rows):
        for j, q in enumerate(in_rows):
            a = sign * (q - r) + 1
            if 0 <= a <= 2:
                table[i, j, a] = 1.0
    return table


ROWS_14 = list(range(-3, 11))
ROWS_12 = list(range(-2, 10))
ROWS_10 = list(range(-1, 9))
ROWS_8 = list(range(8))


def silu_pair(v):
    s = 1.0 / (1.0 + jnp.exp(-v))
    return v * s, s * (1.0 + v * (1.0 - s))


def shifted(v, delta):
    width = v.shape[1]
    lane = lax.broadcasted_iota(jnp.int32, v.shape, 1)
    if delta == 1:
        return jnp.where(lane < width - 1, pltpu.roll(v, width - 1, 1), 0.0)
    return jnp.where(lane > 0, pltpu.roll(v, 1, 1), 0.0)


def nt_dot(a, b):
    return lax.dot_general(a, b, (((1,), (1,)), ((), ())), preferred_element_type=F32)


def denoise_kernel(
    n, scale,
    ds_ref, cot_ref, w1_ref, wm_ref, wl_ref, wlt_ref, wmt_ref, wf_ref,
    den_ref, gd_ref, pg_ref,
    wmb, wmtb, f3, c3, pre1, x3, pm, z3, bfr, d24, gm_acc, gf_acc, gl_acc,
):
    me = lax.axis_index("rows")
    width = ds_ref.shape[1]
    step = 512 if width % 512 == 0 else 128
    chunks = width // step
    first, last = me == 0, me == n - 1

    def valid(row):
        below = jnp.logical_and(row < 0, first)
        above = jnp.logical_and(row >= BAND, last)
        return jnp.logical_not(jnp.logical_or(below, above))

    wmb[...] = jnp.zeros_like(wmb)
    wmtb[...] = jnp.zeros_like(wmtb)
    for b in range(3):
        for r in range(12):
            wmb[r * 32 : r * 32 + 32, b * 448 + r * 32 : b * 448 + r * 32 + 96] = wm_ref[:, b * 96 : b * 96 + 96]
        for r in range(10):
            wmtb[r * 32 : r * 32 + 32, b * 384 + r * 32 : b * 384 + r * 32 + 96] = wmt_ref[:, b * 96 : b * 96 + 96]

    sub = lax.broadcasted_iota(jnp.int32, (16, width), 0)
    outside = jnp.logical_or(
        jnp.logical_and(jnp.logical_and(sub >= 8, sub < 12), first),
        jnp.logical_and(sub >= 12, last),
    )
    ds = jnp.where(outside, 0.0, ds_ref[...])
    cot = jnp.where(outside, 0.0, cot_ref[...])
    f3[0:16, :] = shifted(ds, -1).astype(BF16)
    f3[16:32, :] = ds.astype(BF16)
    f3[32:48, :] = shifted(ds, 1).astype(BF16)
    c3[0:16, :] = shifted(cot, 1).astype(BF16)
    c3[16:32, :] = cot.astype(BF16)
    c3[32:48, :] = shifted(cot, -1).astype(BF16)

    def at(i):
        return pl.ds(pl.multiple_of(i * step, step), step)

    def grp(i):
        return pl.ds(pl.multiple_of(i * 32, 32), 32)

    @pl.loop(0, chunks)
    def _(i):
        pre1[:, at(i)] = jnp.dot(w1_ref[...], f3[:, at(i)], preferred_element_type=F32).astype(pre1.dtype)

    @pl.loop(0, 14)
    def _(r):
        act, slope = silu_pair(pre1[grp(r), :].astype(F32))
        act = jnp.where(valid(r - 3), act, 0.0)
        pre1[grp(r), :] = slope.astype(pre1.dtype)
        x3[grp(r), :] = shifted(act, -1).astype(BF16)
        x3[grp(r + 14), :] = act.astype(BF16)
        x3[grp(r + 28), :] = shifted(act, 1).astype(BF16)

    @pl.loop(0, chunks)
    def _(i):
        pm[:, at(i)] = jnp.dot(wmb[...], x3[:, at(i)], preferred_element_type=F32).astype(pm.dtype)

    @pl.loop(0, 12)
    def _(r):
        act, slope = silu_pair(pm[grp(r), :].astype(F32))
        act = jnp.where(valid(r - 2), act, 0.0)
        slope = jnp.where(valid(r - 2), slope, 0.0)
        pm[grp(r), :] = slope.astype(pm.dtype)
        z3[grp(r), :] = act.astype(BF16)

    gl_acc[...] = jnp.zeros_like(gl_acc)

    @pl.loop(0, chunks)
    def _(i):
        part = z3[32:352, at(i)]
        d24[:, at(i)] = jnp.dot(wl_ref[...], part, preferred_element_type=F32)
        gl_acc[...] += nt_dot(c3[:, at(i)], part)
        back = pm[:, at(i)].astype(F32) * jnp.dot(wlt_ref[...], c3[:, at(i)], preferred_element_type=F32)
        pm[:, at(i)] = back.astype(pm.dtype)

    den_ref[...] = ds_ref[0:8, :] + d24[8:16, :] + shifted(d24[0:8, :], -1) + shifted(d24[16:24, :], 1)

    @pl.loop(0, 12)
    def _(r):
        back = pm[grp(r), :].astype(F32)
        z3[grp(r), :] = shifted(back, 1).astype(BF16)
        z3[grp(r + 12), :] = back.astype(BF16)
        z3[grp(r + 24), :] = shifted(back, -1).astype(BF16)

    gm_acc[...] = jnp.zeros_like(gm_acc)
    gf_acc[...] = jnp.zeros_like(gf_acc)
    row = lax.broadcasted_iota(jnp.int32, (320, step), 0)
    gone = jnp.logical_or(jnp.logical_and(row < 32, first), jnp.logical_and(row >= 288, last))

    @pl.loop(0, chunks)
    def _(i):
        back = jnp.dot(wmtb[...], z3[:, at(i)], preferred_element_type=F32) * pre1[64:384, at(i)].astype(F32)
        back = jnp.where(gone, 0.0, back).astype(BF16)
        bfr[...] = back
        d24[:, at(i)] = jnp.dot(wf_ref[...], back, preferred_element_type=F32)
        gf_acc[...] += nt_dot(bfr[32:288, :], f3[:, at(i)])
        errors = z3[384 + 64 : 384 + 320, at(i)]
        for b in range(3):
            gm_acc[b] += nt_dot(errors, x3[b * 448 + 64 : b * 448 + 384, at(i)])

    gd_ref[...] = cot_ref[0:8, :] + d24[8:16, :] + shifted(d24[0:8, :], 1) + shifted(d24[16:24, :], -1)

    pg_ref[...] = jnp.zeros_like(pg_ref)
    for a in range(3):
        for b in range(3):
            total = gm_acc[b, 0:32, a * 32 : a * 32 + 32]
            for r in range(1, 8):
                total = total + gm_acc[b, r * 32 : r * 32 + 32, (r + a) * 32 : (r + a) * 32 + 32]
            slot = a * 3 + b
            pg_ref[slot // 4 * 32 : slot // 4 * 32 + 32, slot % 4 * 32 : slot % 4 * 32 + 32] = total * scale
            total_first = jnp.zeros((32, 1), F32)
            total_last = jnp.zeros((1, 32), F32)
            for r in range(8):
                col = b * 16 + EXT_ROWS.index(r + a - 1)
                total_first = total_first + gf_acc[r * 32 : r * 32 + 32, col : col + 1]
                total_last = total_last + gl_acc[b * 16 + r : b * 16 + r + 1, (r + a) * 32 : (r + a) * 32 + 32]
            pg_ref[64:96, 32 + slot : 33 + slot] = total_first * scale
            pg_ref[64 + slot : 65 + slot, 64:96] = total_last * scale


def denoise(n, scale, ds_ext, cot_ext, w_first, w_mid, w_last):
    width = ds_ext.shape[1]
    keep = F32 if width <= 4096 else BF16
    wf, wl = w_first[:, 0], w_last[0]

    def ein(spec, table, weight, shape):
        return jnp.einsum(spec, jnp.asarray(table, BF16), weight, preferred_element_type=F32).astype(BF16).reshape(shape)

    w1 = ein("rea,oab->robe", band_select(ROWS_14, EXT_ROWS, 1), wf, (448, 48))
    wl3 = ein("rea,cab->brec", band_select(ROWS_8, ROWS_10, 1), wl, (24, 320))
    wlt = ein("rea,cab->rcbe", band_select(ROWS_12, EXT_ROWS, -1), wl, (384, 48))
    wf3 = ein("rea,oab->breo", band_select(ROWS_8, ROWS_10, -1), wf, (24, 320))
    wm = jnp.transpose(w_mid, (0, 3, 2, 1)).reshape(32, 288)
    wmt = jnp.transpose(jnp.flip(w_mid, 2), (1, 3, 2, 0)).reshape(32, 288)
    return pl.pallas_call(
        functools.partial(denoise_kernel, n, scale),
        out_shape=(
            jax.ShapeDtypeStruct((8, width), F32),
            jax.ShapeDtypeStruct((8, width), F32),
            jax.ShapeDtypeStruct((8 * n, 128), F32),
        ),
        in_specs=[pl.BlockSpec(memory_space=pltpu.VMEM)] * 8,
        out_specs=[pl.BlockSpec(memory_space=pltpu.VMEM)] * 3,
        scratch_shapes=[
            pltpu.VMEM((384, 1344), BF16),
            pltpu.VMEM((320, 1152), BF16),
            pltpu.VMEM((48, width), BF16),
            pltpu.VMEM((48, width), BF16),
            pltpu.VMEM((448, width), keep),
            pltpu.VMEM((1344, width), BF16),
            pltpu.VMEM((384, width), keep),
            pltpu.VMEM((1152, width), BF16),
            pltpu.VMEM((320, 512 if width % 512 == 0 else 128), BF16),
            pltpu.VMEM((24, width), F32),
            pltpu.VMEM((3, 256, 320), F32),
            pltpu.VMEM((256, 48), F32),
            pltpu.VMEM((48, 320), F32),
        ],
        compiler_params=pltpu.CompilerParams(vmem_limit_bytes=60 << 20 if width <= 2048 else 63 << 20),
    )(ds_ext, cot_ext, w1, wm, wl3, wlt, wmt, wf3)


def blur_step(n, with_target, *refs):
    refs = list(refs)
    take = lambda count: [refs.pop(0) for _ in range(count)]
    values_ref, tab_ref = take(2)
    extra_ref, = take(1)
    side_ref = take(1)[0] if with_target else None
    out_ref, other_ref = take(2)
    (send1, cols, padded, adj, send2, back, hx_send, hx_recv,
     s1, r1, s2, r2, hs, hr) = refs
    me = lax.axis_index("rows")
    width = values_ref.shape[1]
    height = BAND * n
    blocks = height // BLK

    def peer(k):
        return lax.rem(me + k, n)

    barrier = pltpu.get_barrier_semaphore()
    for k in range(1, n):
        pl.semaphore_signal(barrier, inc=1, device_id={"rows": peer(k)}, device_id_type=MESH)

    values = values_ref[...]
    wide = jnp.concatenate([values, jnp.zeros((BAND, BLK), F32)], axis=1)
    blurred = jnp.zeros((BAND, width), F32)
    for t in range(TAPS):
        moved = wide if t == RAD else pltpu.roll(wide, (RAD - t) % (width + BLK), 1)
        blurred = blurred + tab_ref[t : t + 1, 0:width] * moved[:, 0:width]
    for j in range(n):
        send1[j, 0:8, :] = blurred[:, j * BLK : j * BLK + BLK]
    if not with_target:
        for j in range(n):
            send1[j, 8:16, :] = extra_ref[j * 8 : j * 8 + 8, :]
    else:
        hx_send[0, 0:4, :] = values[4:8, :]
        hx_send[0, 4:8, :] = extra_ref[4:8, :]
        hx_send[1, 0:4, :] = values[0:4, :]
        hx_send[1, 4:8, :] = extra_ref[0:4, :]
    pl.semaphore_wait(barrier, n - 1)

    def exchange(src, dst, send_sem, recv_sem):
        copies = []
        for k in range(1, n):
            to = peer(k)
            copies.append(pltpu.make_async_remote_copy(
                src_ref=src.at[to], dst_ref=dst.at[me], send_sem=send_sem.at[k - 1], recv_sem=recv_sem.at[k - 1],
                device_id={"rows": to}, device_id_type=MESH))
        for copy in copies:
            copy.start()
        return copies

    first = exchange(send1, cols, s1, r1)
    near = []
    if with_target:
        for side, k in ((0, 1), (1, n - 1)):
            near.append(pltpu.make_async_remote_copy(
                src_ref=hx_send.at[side], dst_ref=hx_recv.at[side], send_sem=hs.at[side], recv_sem=hr.at[side],
                device_id={"rows": peer(k)}, device_id_type=MESH))
        for copy in near:
            copy.start()
    cols[me] = send1[me]
    for copy in first:
        copy.wait_recv()

    padded[...] = jnp.zeros_like(padded)
    for i in range(n):
        padded[16 + i * 8 : 24 + i * 8, :] = cols[i, 0:8, :]
    adj[...] = jnp.zeros_like(adj)
    results = []
    for blk in range(blocks):
        lanes = slice(width + BLK + blk * BLK, width + 2 * BLK + blk * BLK)
        total = jnp.zeros((BLK, BLK), F32)
        for t in range(TAPS):
            start = 16 + blk * BLK + t - RAD
            total = total + tab_ref[t : t + 1, lanes] * padded[start : start + BLK, :]
        if with_target:
            total = total - side_ref[blk * BLK : blk * BLK + BLK, :]
        results.append(total)
    padded[...] = jnp.zeros_like(padded)
    for blk in range(blocks):
        lanes = slice(width + BLK + blk * BLK, width + 2 * BLK + blk * BLK)
        padded[32 : 32 + BLK, :] = results[blk]
        total = jnp.zeros((BLK + 32, BLK), F32)
        for t in range(TAPS):
            start = 16 - t + RAD
            total = total + tab_ref[t : t + 1, lanes] * padded[start : start + BLK + 32, :]
        adj[blk * BLK : blk * BLK + BLK + 32, :] = adj[blk * BLK : blk * BLK + BLK + 32, :] + total
    adj[0:16, :] = jnp.zeros((16, BLK), F32)
    adj[16 + height : 32 + height, :] = jnp.zeros((16, BLK), F32)
    if with_target:
        sub = lax.broadcasted_iota(jnp.int32, (BAND, BLK), 0)
    else:
        share = cols[0, 8:16, :]
        for i in range(1, n):
            share = share + cols[i, 8:16, :]
    for i in range(n):
        base = 16 + i * 8
        send2[i, 0:8, :] = adj[base : base + 8, :]
        if with_target:
            send2[i, 8:16, :] = jnp.where(sub < 4, adj[base - 4 : base + 4, :], adj[base + 4 : base + 12, :])
        else:
            send2[i, 8:16, :] = share
    second = exchange(send2, back, s2, r2)
    back[me] = send2[me]
    for copy in second:
        copy.wait_recv()

    rows = 16 if with_target else 8
    pieces = [back[j, 0:rows, :] for j in range(n)] + [jnp.zeros((rows, BLK), F32)]
    wide = jnp.concatenate(pieces, axis=1)
    table_end = width + BLK
    total = jnp.zeros((rows, table_end), F32)
    for t in range(TAPS):
        part = tab_ref[t : t + 1, 0:table_end] * wide
        total = total + (part if t == RAD else pltpu.roll(part, (t - RAD) % table_end, 1))
    total = total[:, 0:width]
    if with_target:
        for copy in near:
            copy.wait_recv()
        out_ref[0:8, :] = values - STEP_SIZE * total[0:8, :]
        ends = jnp.concatenate([hx_recv[0, 0:4, :], hx_recv[1, 0:4, :]], axis=0)
        out_ref[8:16, :] = ends - STEP_SIZE * total[8:16, :]
        other_ref[0:8, :] = extra_ref[...]
        other_ref[8:16, :] = jnp.concatenate([hx_recv[0, 4:8, :], hx_recv[1, 4:8, :]], axis=0)
    else:
        out_ref[...] = values - STEP_SIZE * total
        for i in range(n):
            other_ref[i * 8 : i * 8 + 8, :] = back[i, 8:16, :]
    for copy in first + near + second:
        copy.wait_send()


def data_gradient(n, values, table, extra, observed):
    width = values.shape[1]
    with_target = observed is not None
    height = BAND * n
    deep = 16 if (with_target or extra is not None) else 8
    rows1 = 8 if with_target else deep
    args = (values, table, extra) + ((observed,) if with_target else ())
    if with_target:
        outs = (jax.ShapeDtypeStruct((16, width), F32), jax.ShapeDtypeStruct((16, width), F32))
    else:
        outs = (jax.ShapeDtypeStruct((8, width), F32), jax.ShapeDtypeStruct((8 * n, BLK), F32))
    return pl.pallas_call(
        functools.partial(blur_step, n, with_target),
        out_shape=outs,
        in_specs=[pl.BlockSpec(memory_space=pltpu.VMEM)] * len(args),
        out_specs=[pl.BlockSpec(memory_space=pltpu.VMEM)] * 2,
        scratch_shapes=[
            pltpu.VMEM((n, rows1, BLK), F32),
            pltpu.VMEM((n, rows1, BLK), F32),
            pltpu.VMEM((max(height, BLK) + 64, BLK), F32),
            pltpu.VMEM((height + 32, BLK), F32),
            pltpu.VMEM((n, deep, BLK), F32),
            pltpu.VMEM((n, deep, BLK), F32),
            pltpu.VMEM((2, 8, width if with_target else BLK), F32),
            pltpu.VMEM((2, 8, width if with_target else BLK), F32),
            pltpu.SemaphoreType.DMA((n - 1,)),
            pltpu.SemaphoreType.DMA((n - 1,)),
            pltpu.SemaphoreType.DMA((n - 1,)),
            pltpu.SemaphoreType.DMA((n - 1,)),
            pltpu.SemaphoreType.DMA((2,)),
            pltpu.SemaphoreType.DMA((2,)),
        ],
        compiler_params=pltpu.CompilerParams(
            collective_id=0 if with_target else 1, has_side_effects=True, vmem_limit_bytes=40 << 20),
    )(*args)


def tap_tables(zone_map, bank_pick, psf_bank, n, position, width, group_cols):
    norm_bank = psf_bank / jnp.sum(psf_bank, axis=1, keepdims=True)
    row_line = lax.dynamic_slice_in_dim(zone_map, position * BAND // BLK, 1, 0)[0]
    col_line = lax.dynamic_slice_in_dim(zone_map, position * group_cols // BLK, 1, 1)[:, 0]

    def pick(line, picks):
        zone = jnp.sum(jnp.where(line[:, None] == jnp.arange(picks.shape[0])[None, :], picks[None, :], 0), axis=1)
        hot = zone[None, :, None] == jnp.arange(psf_bank.shape[0])[None, None, :]
        return jnp.sum(jnp.where(hot, norm_bank.T[:, None, :], 0.0), axis=2)

    per_block = jnp.concatenate(
        [pick(row_line, bank_pick[0]), jnp.zeros((TAPS, 1), F32), pick(col_line, bank_pick[1])], axis=1)
    count = per_block.shape[1]
    return jnp.broadcast_to(per_block[:, :, None], (TAPS, count, BLK)).reshape(TAPS, count * BLK)


def on_device(n, estimate, observed, cotangent, zone_map, bank_pick, psf_bank, w_first, w_mid, w_last):
    width, group_cols = estimate.shape[1], observed.shape[1]
    position = lax.axis_index("rows")
    height = BAND * n
    scale = GRAD_FACTOR / math.sqrt(height * width)
    table = tap_tables(zone_map, bank_pick, psf_bank, n, position, width, group_cols)
    ds_ext, cot_ext = data_gradient(n, estimate, table, cotangent, observed)
    denoised, grad_data, shares = denoise(n, scale, ds_ext, cot_ext, w_first, w_mid, w_last)
    grad_estimate, sums = data_gradient(n, grad_data, table, shares, None)
    slots = sums[0:96].reshape(3, 32, 4, 32)
    grad_mid = jnp.transpose(slots, (1, 3, 0, 2)).reshape(32, 32, 12)[:, :, 0:9].reshape(32, 32, 3, 3)
    grad_first = sums[64:96, 32:41].reshape(32, 1, 3, 3)
    grad_last = jnp.transpose(sums[64:73, 64:96]).reshape(1, 32, 3, 3)
    return denoised, grad_estimate, grad_first, grad_mid, grad_last


def solution(mesh):
    placed = (
        P(("parts", "rows"), None),
        P("parts", "rows"),
        P(("parts", "rows"), None),
        P("parts", None),
        P(), P(), P(), P(), P(),
    )
    return jax.shard_map(
        functools.partial(on_device, mesh.shape["rows"]),
        mesh=mesh,
        in_specs=placed,
        out_specs=(
            P(("parts", "rows"), None),
            P(("parts", "rows"), None),
            P("parts", None, None, None),
            P("parts", None, None, None),
            P("parts", None, None, None),
        ),
        check_vma=False,
    )
```

```python
import functools
import math

import jax
import jax.numpy as jnp
from jax import lax
from jax.experimental import pallas as pl
from jax.experimental.pallas import tpu as pltpu
from jax.sharding import PartitionSpec as P

BLK = 128
RAD = 12
TAPS = 2 * RAD + 1
CH = 32
BAND = 8
STEP_SIZE = 2.0
GRAD_FACTOR = 8.0
MESH = pl.DeviceIdType.MESH
F32 = jnp.float32
BF16 = jnp.bfloat16

EXT_ROWS = list(range(8)) + [-4, -3, -2, -1, 8, 9, 10, 11]


ROWS_14 = list(range(-3, 11))
ROWS_12 = list(range(-2, 10))
ROWS_10 = list(range(-1, 9))
ROWS_8 = list(range(8))


def silu_pair(v):
    s = 0.5 * jnp.tanh(0.5 * v) + 0.5
    return v * s, s * (1.0 + v * (1.0 - s))


def shifted(v, delta):
    width = v.shape[1]
    lane = lax.broadcasted_iota(jnp.int32, v.shape, 1)
    if delta == 1:
        return jnp.where(lane < width - 1, pltpu.roll(v, width - 1, 1), 0.0)
    return jnp.where(lane > 0, pltpu.roll(v, 1, 1), 0.0)


def nt_dot(a, b):
    return lax.dot_general(a, b, (((1,), (1,)), ((), ())), preferred_element_type=F32)


def iota(shape, dim):
    return lax.broadcasted_iota(jnp.int32, shape, dim)


def third(v, size):
    return (v >= size).astype(jnp.int32) + (v >= 2 * size).astype(jnp.int32)


def ones_where(cond):
    return jnp.where(cond, 1.0, 0.0).astype(BF16)


def build_table(n, tab, zone_ref, pick_ref, psf_ref, hot, blocks_row, blocks_col):
    me = lax.axis_index("rows")
    row = iota((8, BLK), 0)
    for i in range(blocks_row):
        k = pick_ref[0, zone_ref[me * BAND // BLK, i]]
        hot[:, i * BLK : i * BLK + BLK] = jnp.where(row == k, 1.0, 0.0)
    hot[:, blocks_row * BLK : blocks_row * BLK + BLK] = jnp.zeros((8, BLK), F32)
    for i in range(blocks_col):
        k = pick_ref[1, zone_ref[i, me]]
        at = (blocks_row + 1 + i) * BLK
        hot[:, at : at + BLK] = jnp.where(row == k, 1.0, 0.0)
    psf = psf_ref[...]
    norm = psf / jnp.sum(psf, axis=1, keepdims=True)
    tab[0:TAPS, :] = lax.dot_general(
        norm, hot[...], (((0,), (0,)), ((), ())), preferred_element_type=F32, precision=lax.Precision.HIGHEST)


def build_weights(wf_ref, wl_ref, w2_ref, wsel, w1, wlt, wl3, wf3, wmb, wmtb):
    k, lane = iota((9, 48), 0), iota((9, 48), 1)
    ka = third(k, 3)
    kb = k - 3 * ka
    lb = third(lane, 16)
    le = lane - 16 * lb
    same = kb == lb

    def select(row, sign):
        hit = None
        for a in range(3):
            q = row + sign * (a - 1)
            if q in EXT_ROWS:
                here = jnp.logical_and(ka == a, le == EXT_ROWS.index(q))
                hit = here if hit is None else jnp.logical_or(hit, here)
        return ones_where(jnp.logical_and(same, hit))

    for i, r in enumerate(ROWS_14):
        w1[i * 32 : i * 32 + 32, :] = jnp.dot(wf_ref[...], select(r, 1), preferred_element_type=F32).astype(BF16)
    for i, r in enumerate(ROWS_12):
        wlt[i * 32 : i * 32 + 32, :] = jnp.dot(wl_ref[...], select(r, -1), preferred_element_type=F32).astype(BF16)
    out, k = iota((24, 9), 0), iota((24, 9), 1)
    ob = third(out, 8)
    orow = out - 8 * ob
    ka = third(k, 3)
    same = k - 3 * ka == ob
    for i, q in enumerate(ROWS_10):
        fwd = ones_where(jnp.logical_and(same, ka == q - orow + 1))
        wl3[:, i * 32 : i * 32 + 32] = nt_dot(fwd, wl_ref[...]).astype(BF16)
        adj = ones_where(jnp.logical_and(same, ka == orow - q + 1))
        wf3[:, i * 32 : i * 32 + 32] = nt_dot(adj, wf_ref[...]).astype(BF16)
    k, m = iota((288, 288), 0), iota((288, 288), 1)
    mb = third(m, 96)
    rest = m - 96 * mb
    ma = third(rest, 32)
    order = ones_where(k == (rest - 32 * ma) * 9 + ma * 3 + mb)
    wm = jnp.dot(w2_ref[...], order, preferred_element_type=F32).astype(BF16)
    wsel[...] = wm
    eye = ones_where(iota((32, 32), 0) == iota((32, 32), 1))
    wmb[...] = jnp.zeros_like(wmb)
    wmtb[...] = jnp.zeros_like(wmtb)
    for b in range(3):
        for r in range(12):
            wmb[r * 32 : r * 32 + 32, b * 448 + r * 32 : b * 448 + r * 32 + 96] = wsel[:, b * 96 : b * 96 + 96]
        turned = [nt_dot(eye, wsel[:, b * 96 + (2 - a) * 32 : b * 96 + (2 - a) * 32 + 32]) for a in range(3)]
        turned = jnp.concatenate(turned, axis=1).astype(BF16)
        for r in range(10):
            wmtb[r * 32 : r * 32 + 32, b * 384 + r * 32 : b * 384 + r * 32 + 96] = turned


def row_blur(values, tab):
    width = values.shape[1]
    wide = jnp.concatenate([values, jnp.zeros((BAND, BLK), F32)], axis=1)
    blurred = jnp.zeros((BAND, width), F32)
    for t in range(TAPS):
        moved = wide if t == RAD else pltpu.roll(wide, (RAD - t) % (width + BLK), 1)
        blurred = blurred + tab[t : t + 1, 0:width] * moved[:, 0:width]
    return blurred


def row_blur_adjoint(back, rows, n, width, tab):
    end = width + BLK
    wide = jnp.concatenate([back[j] for j in range(n)] + [jnp.zeros((rows, BLK), F32)], axis=1)
    total = jnp.zeros((rows, end), F32)
    for t in range(TAPS):
        part = tab[t : t + 1, 0:end] * wide
        total = total + (part if t == RAD else pltpu.roll(part, (t - RAD) % end, 1))
    return total[:, 0:width]


def column_pass(n, width, cols, padded, adj, tab, target):
    height = BAND * n
    blocks = height // BLK
    padded[...] = jnp.zeros_like(padded)
    for i in range(n):
        padded[16 + i * 8 : 24 + i * 8, :] = cols[i]
    results = []
    for blk in range(blocks):
        lanes = slice(width + (blk + 1) * BLK, width + (blk + 2) * BLK)
        total = jnp.zeros((BLK, BLK), F32)
        for t in range(TAPS):
            start = 16 + blk * BLK + t - RAD
            total = total + tab[t : t + 1, lanes] * padded[start : start + BLK, :]
        if target is not None:
            total = total - target[blk * BLK : blk * BLK + BLK, :]
        results.append(total)
    padded[...] = jnp.zeros_like(padded)
    adj[...] = jnp.zeros_like(adj)
    for blk in range(blocks):
        lanes = slice(width + (blk + 1) * BLK, width + (blk + 2) * BLK)
        padded[32 : 32 + BLK, :] = results[blk]
        total = jnp.zeros((BLK + 32, BLK), F32)
        for t in range(TAPS):
            start = 16 - t + RAD
            total = total + tab[t : t + 1, lanes] * padded[start : start + BLK + 32, :]
        adj[blk * BLK : blk * BLK + BLK + 32, :] = adj[blk * BLK : blk * BLK + BLK + 32, :] + total
    adj[0:16, :] = jnp.zeros((16, BLK), F32)
    adj[16 + height : 32 + height, :] = jnp.zeros((16, BLK), F32)


def kernel(
    n, scale,
    est_ref, obs_ref, cot_in_ref, zone_ref, pick_ref, psf_ref, wf_ref, wl_ref, w2_ref,
    den_ref, ge_ref, sums_ref,
    tab, hot, send1, cols1, send2, back2, send3, cols3, send4, back4, share, share_in, whole, padded, adj,
    hx_send, hx_recv, ds_ref, cot_ref,
    wsel, w1, wlt, wl3, wf3, wmb, wmtb, f3, c3, pre1, x3, pm, mid, bfr, d24, gm_acc, gf_acc, gl_acc,
    send_sems, recv_sems, hs, hr,
):
    me = lax.axis_index("rows")
    width = est_ref.shape[1]
    step = bfr.shape[1]
    chunks = width // step
    first, last = me == 0, me == n - 1
    started = []

    def peer(k):
        return lax.rem(me + k, n)

    barrier = pltpu.get_barrier_semaphore()
    for k in range(1, n):
        pl.semaphore_signal(barrier, inc=1, device_id={"rows": peer(k)}, device_id_type=MESH)

    def exchange(index, src_at, dst):
        copies = []
        for k in range(1, n):
            to = peer(k)
            copies.append(pltpu.make_async_remote_copy(
                src_ref=src_at(to), dst_ref=dst.at[me],
                send_sem=send_sems.at[index, k - 1], recv_sem=recv_sems.at[index, k - 1],
                device_id={"rows": to}, device_id_type=MESH))
        for copy in copies:
            copy.start()
        started.extend(copies)
        return copies

    def arrive(copies):
        for copy in copies:
            copy.wait_recv()

    build_table(n, tab, zone_ref, pick_ref, psf_ref, hot, width // BLK, BAND * n // BLK)
    blurred = row_blur(est_ref[...], tab)
    for j in range(n):
        send1[j] = blurred[:, j * BLK : j * BLK + BLK]
    hx_send[0, 0:4, :] = est_ref[4:8, :]
    hx_send[0, 4:8, :] = cot_in_ref[4:8, :]
    hx_send[1, 0:4, :] = est_ref[0:4, :]
    hx_send[1, 4:8, :] = cot_in_ref[0:4, :]
    pl.semaphore_wait(barrier, n - 1)
    copies1 = exchange(0, lambda to: send1.at[to], cols1)
    near = []
    for side, k in ((0, 1), (1, n - 1)):
        near.append(pltpu.make_async_remote_copy(
            src_ref=hx_send.at[side], dst_ref=hx_recv.at[side], send_sem=hs.at[side], recv_sem=hr.at[side],
            device_id={"rows": peer(k)}, device_id_type=MESH))
    for copy in near:
        copy.start()
    cols1[me] = send1[me]
    build_weights(wf_ref, wl_ref, w2_ref, wsel, w1, wlt, wl3, wf3, wmb, wmtb)
    arrive(copies1)
    column_pass(n, width, cols1, padded, adj, tab, obs_ref)
    sub = iota((BAND, BLK), 0)
    for i in range(n):
        base = 16 + i * 8
        send2[i, 0:8, :] = adj[base : base + 8, :]
        send2[i, 8:16, :] = jnp.where(sub < 4, adj[base - 4 : base + 4, :], adj[base + 4 : base + 12, :])
    copies2 = exchange(1, lambda to: send2.at[to], back2)
    back2[me] = send2[me]

    sub = iota((16, width), 0)
    outside = jnp.logical_or(
        jnp.logical_and(jnp.logical_and(sub >= 8, sub < 12), first), jnp.logical_and(sub >= 12, last))
    arrive(near)
    cot_ref[0:8, :] = cot_in_ref[...]
    cot_ref[8:12, :] = hx_recv[0, 4:8, :]
    cot_ref[12:16, :] = hx_recv[1, 4:8, :]
    ds_ref[0:8, :] = est_ref[...]
    ds_ref[8:12, :] = hx_recv[0, 0:4, :]
    ds_ref[12:16, :] = hx_recv[1, 0:4, :]
    cot = jnp.where(outside, 0.0, cot_ref[...])
    c3[0:16, :] = shifted(cot, 1).astype(BF16)
    c3[16:32, :] = cot.astype(BF16)
    c3[32:48, :] = shifted(cot, -1).astype(BF16)
    arrive(copies2)

    ds = ds_ref[...] - STEP_SIZE * row_blur_adjoint(back2, 16, n, width, tab)
    ds = jnp.where(outside, 0.0, ds)
    ds_ref[...] = ds
    f3[0:16, :] = shifted(ds, -1).astype(BF16)
    f3[16:32, :] = ds.astype(BF16)
    f3[32:48, :] = shifted(ds, 1).astype(BF16)

    def valid(row):
        below = jnp.logical_and(row < 0, first)
        above = jnp.logical_and(row >= BAND, last)
        return jnp.logical_not(jnp.logical_or(below, above))

    def at(i):
        return pl.ds(pl.multiple_of(i * step, step), step)

    def grp(i):
        return pl.ds(pl.multiple_of(i * 32, 32), 32)

    @pl.loop(0, chunks)
    def _(i):
        pre1[:, at(i)] = jnp.dot(w1[...], f3[:, at(i)], preferred_element_type=F32).astype(pre1.dtype)

    @pl.loop(0, 14)
    def _(r):
        act, slope = silu_pair(pre1[grp(r), :].astype(F32))
        act = jnp.where(valid(r - 3), act, 0.0)
        pre1[grp(r), :] = slope.astype(pre1.dtype)
        x3[grp(r), :] = shifted(act, -1).astype(BF16)
        x3[grp(r + 14), :] = act.astype(BF16)
        x3[grp(r + 28), :] = shifted(act, 1).astype(BF16)

    @pl.loop(0, chunks)
    def _(i):
        pm[:, at(i)] = jnp.dot(wmb[...], x3[:, at(i)], preferred_element_type=F32).astype(pm.dtype)

    @pl.loop(0, 12)
    def _(r):
        act, slope = silu_pair(pm[grp(r), :].astype(F32))
        act = jnp.where(valid(r - 2), act, 0.0)
        slope = jnp.where(valid(r - 2), slope, 0.0)
        pm[grp(r), :] = slope.astype(pm.dtype)
        mid[grp(r), :] = act.astype(BF16)

    gl_acc[...] = jnp.zeros_like(gl_acc)

    @pl.loop(0, chunks)
    def _(i):
        part = mid[32:352, at(i)]
        d24[:, at(i)] = jnp.dot(wl3[...], part, preferred_element_type=F32)
        gl_acc[...] += nt_dot(c3[:, at(i)], part)
        back = pm[:, at(i)].astype(F32) * jnp.dot(wlt[...], c3[:, at(i)], preferred_element_type=F32)
        pm[:, at(i)] = back.astype(pm.dtype)

    den_ref[...] = ds_ref[0:8, :] + d24[8:16, :] + shifted(d24[0:8, :], -1) + shifted(d24[16:24, :], 1)

    @pl.loop(0, 12)
    def _(r):
        back = pm[grp(r), :].astype(F32)
        x3[grp(r), :] = shifted(back, 1).astype(BF16)
        mid[grp(r), :] = back.astype(BF16)
        x3[grp(r + 28), :] = shifted(back, -1).astype(BF16)

    gf_acc[...] = jnp.zeros_like(gf_acc)
    row = iota((320, step), 0)
    gone = jnp.logical_or(jnp.logical_and(row < 32, first), jnp.logical_and(row >= 288, last))

    @pl.loop(0, chunks)
    def _(i):
        back = (
            jnp.dot(wmtb[:, 0:384], x3[0:384, at(i)], preferred_element_type=F32)
            + jnp.dot(wmtb[:, 384:768], mid[:, at(i)], preferred_element_type=F32)
            + jnp.dot(wmtb[:, 768:1152], x3[896:1280, at(i)], preferred_element_type=F32)
        ) * pre1[64:384, at(i)].astype(F32)
        back = jnp.where(gone, 0.0, back).astype(BF16)
        bfr[...] = back
        d24[:, at(i)] = jnp.dot(wf3[...], back, preferred_element_type=F32)
        gf_acc[...] += nt_dot(bfr[32:288, :], f3[:, at(i)])

    ge_ref[...] = cot_ref[0:8, :] + d24[8:16, :] + shifted(d24[0:8, :], 1) + shifted(d24[16:24, :], -1)
    blurred = row_blur(ge_ref[...], tab)
    for j in range(n):
        send3[j] = blurred[:, j * BLK : j * BLK + BLK]
    copies3 = exchange(2, lambda to: send3.at[to], cols3)
    cols3[me] = send3[me]

    gm_acc[...] = jnp.zeros_like(gm_acc)

    @pl.loop(0, chunks)
    def _(i):
        act = x3[448 + 64 : 448 + 384, at(i)]
        gm_acc[0] += nt_dot(x3[64:320, at(i)], act)
        gm_acc[1] += nt_dot(mid[64:320, at(i)], act)
        gm_acc[2] += nt_dot(x3[896 + 64 : 896 + 320, at(i)], act)

    share[...] = jnp.zeros_like(share)
    for a in range(3):
        for b in range(3):
            total = gm_acc[b, 0:32, a * 32 : a * 32 + 32]
            for r in range(1, 8):
                total = total + gm_acc[b, r * 32 : r * 32 + 32, (r + a) * 32 : (r + a) * 32 + 32]
            slot = a * 3 + b
            share[slot // 4 * 32 : slot // 4 * 32 + 32, slot % 4 * 32 : slot % 4 * 32 + 32] = total * scale
            total_first = jnp.zeros((32, 1), F32)
            total_last = jnp.zeros((1, 32), F32)
            for r in range(8):
                col = b * 16 + EXT_ROWS.index(r + a - 1)
                total_first = total_first + gf_acc[r * 32 : r * 32 + 32, col : col + 1]
                total_last = total_last + gl_acc[b * 16 + r : b * 16 + r + 1, (r + a) * 32 : (r + a) * 32 + 32]
            share[64:96, 32 + slot : 33 + slot] = total_first * scale
            share[64 + slot : 65 + slot, 64:96] = total_last * scale

    def eight(i):
        return pl.ds(pl.multiple_of(i * 8, 8), 8)

    copies5 = exchange(4, lambda to: share.at[eight(to)], share_in)
    share_in[me] = share[eight(me), :]
    arrive(copies3)
    column_pass(n, width, cols3, padded, adj, tab, None)
    for i in range(n):
        send4[i] = adj[16 + i * 8 : 24 + i * 8, :]
    copies4 = exchange(3, lambda to: send4.at[to], back4)
    back4[me] = send4[me]
    arrive(copies5)
    total = share_in[0]
    for i in range(1, n):
        total = total + share_in[i]
    whole[me] = total
    copies6 = exchange(5, lambda to: whole.at[me], whole)
    arrive(copies4)
    ge_ref[...] = ge_ref[...] - STEP_SIZE * row_blur_adjoint(back4, 8, n, width, tab)
    arrive(copies6)
    for i in range(n):
        sums_ref[i * 8 : i * 8 + 8, :] = whole[i]
    for copy in started + near:
        copy.wait_send()


def on_device(n, estimate, observed, cotangent, zone_map, bank_pick, psf_bank, w_first, w_mid, w_last):
    width = estimate.shape[1]
    height = BAND * n
    scale = GRAD_FACTOR / math.sqrt(height * width)
    keep = F32 if width <= 4096 else BF16
    step = 512 if width % 512 == 0 else BLK
    table = width + BLK + height
    vmem, smem = pl.BlockSpec(memory_space=pltpu.VMEM), pl.BlockSpec(memory_space=pltpu.SMEM)
    block = pltpu.VMEM((n, 8, BLK), F32)
    tall = pltpu.VMEM((n, 16, BLK), F32)
    denoised, grad_estimate, sums = pl.pallas_call(
        functools.partial(kernel, n, scale),
        out_shape=(
            jax.ShapeDtypeStruct((8, width), F32),
            jax.ShapeDtypeStruct((8, width), F32),
            jax.ShapeDtypeStruct((8 * n, BLK), F32),
        ),
        in_specs=[vmem, vmem, vmem, smem, smem, vmem, vmem, vmem, vmem],
        out_specs=[vmem] * 3,
        scratch_shapes=[
            pltpu.VMEM((32, table), F32),
            pltpu.VMEM((8, table), F32),
            block, block, tall, tall, block, block, block, block,
            pltpu.VMEM((8 * n, BLK), F32), block, block,
            pltpu.VMEM((max(height, BLK) + 64, BLK), F32),
            pltpu.VMEM((height + 32, BLK), F32),
            pltpu.VMEM((2, 8, width), F32),
            pltpu.VMEM((2, 8, width), F32),
            pltpu.VMEM((16, width), F32),
            pltpu.VMEM((16, width), F32),
            pltpu.VMEM((32, 288), BF16),
            pltpu.VMEM((448, 48), BF16),
            pltpu.VMEM((384, 48), BF16),
            pltpu.VMEM((24, 320), BF16),
            pltpu.VMEM((24, 320), BF16),
            pltpu.VMEM((384, 1344), BF16),
            pltpu.VMEM((320, 1152), BF16),
            pltpu.VMEM((48, width), BF16),
            pltpu.VMEM((48, width), BF16),
            pltpu.VMEM((448, width), keep),
            pltpu.VMEM((1344, width), BF16),
            pltpu.VMEM((384, width), keep),
            pltpu.VMEM((384, width), BF16),
            pltpu.VMEM((320, step), BF16),
            pltpu.VMEM((24, width), F32),
            pltpu.VMEM((3, 256, 320), F32),
            pltpu.VMEM((256, 48), F32),
            pltpu.VMEM((48, 320), F32),
            pltpu.SemaphoreType.DMA((6, n - 1)),
            pltpu.SemaphoreType.DMA((6, n - 1)),
            pltpu.SemaphoreType.DMA((2,)),
            pltpu.SemaphoreType.DMA((2,)),
        ],
        compiler_params=pltpu.CompilerParams(
            collective_id=0, has_side_effects=True, vmem_limit_bytes=56 << 20 if width <= 4096 else 64 << 20),
    )(estimate, observed, cotangent, zone_map, bank_pick, psf_bank,
      w_first.reshape(32, 9), w_last.reshape(32, 9), w_mid.reshape(32, 288))
    slots = sums[0:96].reshape(3, 32, 4, 32)
    grad_mid = jnp.transpose(slots, (1, 3, 0, 2)).reshape(32, 32, 12)[:, :, 0:9].reshape(32, 32, 3, 3)
    grad_first = sums[64:96, 32:41].reshape(32, 1, 3, 3)
    grad_last = jnp.transpose(sums[64:73, 64:96]).reshape(1, 32, 3, 3)
    return denoised, grad_estimate, grad_first, grad_mid, grad_last


def solution(mesh):
    placed = (
        P(("parts", "rows"), None),
        P("parts", "rows"),
        P(("parts", "rows"), None),
        P("parts", None),
        P(), P(), P(), P(), P(),
    )
    return jax.shard_map(
        functools.partial(on_device, mesh.shape["rows"]),
        mesh=mesh,
        in_specs=placed,
        out_specs=(
            P(("parts", "rows"), None),
            P(("parts", "rows"), None),
            P("parts", None, None, None),
            P("parts", None, None, None),
            P("parts", None, None, None),
        ),
        check_vma=False,
    )
```

```python
import functools
import math

import jax
import jax.numpy as jnp
from jax import lax
from jax.experimental import pallas as pl
from jax.experimental.pallas import tpu as pltpu
from jax.sharding import PartitionSpec as P

BLK = 128
RAD = 12
TAPS = 2 * RAD + 1
CH = 32
BAND = 8
STEP_SIZE = 2.0
GRAD_FACTOR = 8.0
MESH = pl.DeviceIdType.MESH
F32 = jnp.float32
BF16 = jnp.bfloat16

EXT_ROWS = list(range(8)) + [-4, -3, -2, -1, 8, 9, 10, 11]


ROWS_14 = list(range(-3, 11))
ROWS_12 = list(range(-2, 10))
ROWS_10 = list(range(-1, 9))
ROWS_8 = list(range(8))


def silu_pair(v):
    s = 0.5 * jnp.tanh(0.5 * v) + 0.5
    return v * s, s * (1.0 + v * (1.0 - s))


def shifted(v, delta):
    width = v.shape[1]
    lane = lax.broadcasted_iota(jnp.int32, v.shape, 1)
    if delta == 1:
        return jnp.where(lane < width - 1, pltpu.roll(v, width - 1, 1), 0.0)
    return jnp.where(lane > 0, pltpu.roll(v, 1, 1), 0.0)


def put_shifted(ref, rows, v, delta):
    width = v.shape[1]
    edge = width - 1 if delta == 1 else 0
    ref[rows, :] = pltpu.roll(v, width - 1 if delta == 1 else 1, 1).astype(BF16)
    ref[rows, edge : edge + 1] = jnp.zeros((v.shape[0], 1), BF16)


def tn_dot(a, b):
    return lax.dot_general(a, b, (((0,), (0,)), ((), ())), preferred_element_type=F32)


def nt_dot(a, b):
    return lax.dot_general(a, b, (((1,), (1,)), ((), ())), preferred_element_type=F32)


def iota(shape, dim):
    return lax.broadcasted_iota(jnp.int32, shape, dim)


def third(v, size):
    return (v >= size).astype(jnp.int32) + (v >= 2 * size).astype(jnp.int32)


def ones_where(cond):
    return jnp.where(cond, 1.0, 0.0).astype(BF16)


def build_table(n, tab, zone_ref, pick_ref, psf_ref, hot, blocks_row, blocks_col):
    me = lax.axis_index("rows")
    row = iota((8, BLK), 0)
    for i in range(blocks_row):
        k = pick_ref[0, zone_ref[me * BAND // BLK, i]]
        hot[:, i * BLK : i * BLK + BLK] = jnp.where(row == k, 1.0, 0.0)
    hot[:, blocks_row * BLK : blocks_row * BLK + BLK] = jnp.zeros((8, BLK), F32)
    for i in range(blocks_col):
        k = pick_ref[1, zone_ref[i, me]]
        at = (blocks_row + 1 + i) * BLK
        hot[:, at : at + BLK] = jnp.where(row == k, 1.0, 0.0)
    psf = psf_ref[...]
    norm = psf / jnp.sum(psf, axis=1, keepdims=True)
    tab[0:TAPS, :] = lax.dot_general(
        norm, hot[...], (((0,), (0,)), ((), ())), preferred_element_type=F32, precision=lax.Precision.HIGHEST)


def build_weights(wfl_ref, w9_ref, w1, wlt, wl3, wf3, wmb, wmtb):
    wf, wl = wfl_ref[0], wfl_ref[1]
    k, lane = iota((9, 48), 0), iota((9, 48), 1)
    ka = third(k, 3)
    kb = k - 3 * ka
    lb = third(lane, 16)
    le = lane - 16 * lb
    same = kb == lb

    def select(row, sign):
        hit = None
        for a in range(3):
            q = row + sign * (a - 1)
            if q in EXT_ROWS:
                here = jnp.logical_and(ka == a, le == EXT_ROWS.index(q))
                hit = here if hit is None else jnp.logical_or(hit, here)
        return ones_where(jnp.logical_and(same, hit))

    for i, r in enumerate(ROWS_14):
        w1[i * 32 : i * 32 + 32, :] = tn_dot(wf, select(r, 1)).astype(BF16)
    for i, r in enumerate(ROWS_12):
        wlt[i * 32 : i * 32 + 32, :] = tn_dot(wl, select(r, -1)).astype(BF16)
    out, k = iota((24, 9), 0), iota((24, 9), 1)
    ob = third(out, 8)
    orow = out - 8 * ob
    ka = third(k, 3)
    same = k - 3 * ka == ob
    for i, q in enumerate(ROWS_10):
        fwd = ones_where(jnp.logical_and(same, ka == q - orow + 1))
        wl3[:, i * 32 : i * 32 + 32] = jnp.dot(fwd, wl, preferred_element_type=F32).astype(BF16)
        adj = ones_where(jnp.logical_and(same, ka == orow - q + 1))
        wf3[:, i * 32 : i * 32 + 32] = jnp.dot(adj, wf, preferred_element_type=F32).astype(BF16)
    eye = ones_where(iota((32, 32), 0) == iota((32, 32), 1))
    wmb[...] = jnp.zeros_like(wmb)
    wmtb[...] = jnp.zeros_like(wmtb)
    for b in range(3):
        line = jnp.concatenate([w9_ref[a * 3 + b] for a in range(3)], axis=1)
        for r in range(6):
            wmb[r * 32 : r * 32 + 32, b * 256 + r * 32 : b * 256 + r * 32 + 96] = line
        turned = [nt_dot(eye, w9_ref[(2 - a) * 3 + b]) for a in range(3)]
        turned = jnp.concatenate(turned, axis=1).astype(BF16)
        for r in range(5):
            wmtb[r * 32 : r * 32 + 32, b * 256 + r * 32 : b * 256 + r * 32 + 96] = turned


def row_blur(values, tab):
    width = values.shape[1]
    wide = jnp.concatenate([values, jnp.zeros((BAND, BLK), F32)], axis=1)
    blurred = jnp.zeros((BAND, width), F32)
    for t in range(TAPS):
        moved = wide if t == RAD else pltpu.roll(wide, (RAD - t) % (width + BLK), 1)
        blurred = blurred + tab[t : t + 1, 0:width] * moved[:, 0:width]
    return blurred


def row_blur_adjoint(back, rows, n, width, tab):
    end = width + BLK
    wide = jnp.concatenate([back[j] for j in range(n)] + [jnp.zeros((rows, BLK), F32)], axis=1)
    total = jnp.zeros((rows, end), F32)
    for t in range(TAPS):
        part = tab[t : t + 1, 0:end] * wide
        total = total + (part if t == RAD else pltpu.roll(part, (t - RAD) % end, 1))
    return total[:, 0:width]


def column_pass(n, width, cols, padded, adj, tab, target):
    height = BAND * n
    blocks = height // BLK
    padded[...] = jnp.zeros_like(padded)
    for i in range(n):
        padded[16 + i * 8 : 24 + i * 8, :] = cols[i]
    results = []
    for blk in range(blocks):
        lanes = slice(width + (blk + 1) * BLK, width + (blk + 2) * BLK)
        total = jnp.zeros((BLK, BLK), F32)
        for t in range(TAPS):
            start = 16 + blk * BLK + t - RAD
            total = total + tab[t : t + 1, lanes] * padded[start : start + BLK, :]
        if target is not None:
            total = total - target[blk * BLK : blk * BLK + BLK, :]
        results.append(total)
    padded[...] = jnp.zeros_like(padded)
    adj[...] = jnp.zeros_like(adj)
    for blk in range(blocks):
        lanes = slice(width + (blk + 1) * BLK, width + (blk + 2) * BLK)
        padded[32 : 32 + BLK, :] = results[blk]
        total = jnp.zeros((BLK + 32, BLK), F32)
        for t in range(TAPS):
            start = 16 - t + RAD
            total = total + tab[t : t + 1, lanes] * padded[start : start + BLK + 32, :]
        adj[blk * BLK : blk * BLK + BLK + 32, :] = adj[blk * BLK : blk * BLK + BLK + 32, :] + total
    adj[0:16, :] = jnp.zeros((16, BLK), F32)
    adj[16 + height : 32 + height, :] = jnp.zeros((16, BLK), F32)


def kernel(
    n, scale,
    est_ref, obs_ref, cot_in_ref, zone_ref, pick_ref, psf_ref, wfl_ref, w9_ref,
    den_ref, ge_ref, gm_ref, gf_ref, gl_ref,
    tab, hot, send1, cols1, send2, back2, send3, cols3, send4, back4, share, share_in, whole, padded, adj,
    hx_send, hx_recv, ds_ref, cot_ref,
    w1, wlt, wl3, wf3, wmb, wmtb, f3, c3, pre1, x3, pm, mid, bfr, d24, gm_acc, gf_acc, gl_acc,
    send_sems, recv_sems, hs, hr,
):
    me = lax.axis_index("rows")
    width = est_ref.shape[1]
    step = bfr.shape[1]
    chunks = width // step
    first, last = me == 0, me == n - 1
    started = []

    def peer(k):
        return lax.rem(me + k, n)

    barrier = pltpu.get_barrier_semaphore()
    for k in range(1, n):
        pl.semaphore_signal(barrier, inc=1, device_id={"rows": peer(k)}, device_id_type=MESH)

    def exchange(index, src_at, dst):
        copies = []
        for k in range(1, n):
            to = peer(k)
            copies.append(pltpu.make_async_remote_copy(
                src_ref=src_at(to), dst_ref=dst.at[me],
                send_sem=send_sems.at[index, k - 1], recv_sem=recv_sems.at[index, k - 1],
                device_id={"rows": to}, device_id_type=MESH))
        for copy in copies:
            copy.start()
        started.extend(copies)
        return copies

    def arrive(copies):
        for copy in copies:
            copy.wait_recv()

    build_table(n, tab, zone_ref, pick_ref, psf_ref, hot, width // BLK, BAND * n // BLK)
    blurred = row_blur(est_ref[...], tab)
    for j in range(n):
        send1[j] = blurred[:, j * BLK : j * BLK + BLK]
    hx_send[0, 0:4, :] = est_ref[4:8, :]
    hx_send[0, 4:8, :] = cot_in_ref[4:8, :]
    hx_send[1, 0:4, :] = est_ref[0:4, :]
    hx_send[1, 4:8, :] = cot_in_ref[0:4, :]
    pl.semaphore_wait(barrier, n - 1)
    copies1 = exchange(0, lambda to: send1.at[to], cols1)
    near = []
    for side, k in ((0, 1), (1, n - 1)):
        near.append(pltpu.make_async_remote_copy(
            src_ref=hx_send.at[side], dst_ref=hx_recv.at[side], send_sem=hs.at[side], recv_sem=hr.at[side],
            device_id={"rows": peer(k)}, device_id_type=MESH))
    for copy in near:
        copy.start()
    cols1[me] = send1[me]
    build_weights(wfl_ref, w9_ref, w1, wlt, wl3, wf3, wmb, wmtb)
    arrive(copies1)
    column_pass(n, width, cols1, padded, adj, tab, obs_ref)
    sub = iota((BAND, BLK), 0)
    for i in range(n):
        base = 16 + i * 8
        send2[i, 0:8, :] = adj[base : base + 8, :]
        send2[i, 8:16, :] = jnp.where(sub < 4, adj[base - 4 : base + 4, :], adj[base + 4 : base + 12, :])
    copies2 = exchange(1, lambda to: send2.at[to], back2)
    back2[me] = send2[me]

    sub = iota((16, width), 0)
    outside = jnp.logical_or(
        jnp.logical_and(jnp.logical_and(sub >= 8, sub < 12), first), jnp.logical_and(sub >= 12, last))
    arrive(near)
    cot_ref[0:8, :] = cot_in_ref[...]
    cot_ref[8:12, :] = hx_recv[0, 4:8, :]
    cot_ref[12:16, :] = hx_recv[1, 4:8, :]
    ds_ref[0:8, :] = est_ref[...]
    ds_ref[8:12, :] = hx_recv[0, 0:4, :]
    ds_ref[12:16, :] = hx_recv[1, 0:4, :]
    cot = jnp.where(outside, 0.0, cot_ref[...])
    c3[0:16, :] = shifted(cot, 1).astype(BF16)
    c3[16:32, :] = cot.astype(BF16)
    c3[32:48, :] = shifted(cot, -1).astype(BF16)
    arrive(copies2)

    ds = ds_ref[...] - STEP_SIZE * row_blur_adjoint(back2, 16, n, width, tab)
    ds = jnp.where(outside, 0.0, ds)
    ds_ref[...] = ds
    f3[0:16, :] = shifted(ds, -1).astype(BF16)
    f3[16:32, :] = ds.astype(BF16)
    f3[32:48, :] = shifted(ds, 1).astype(BF16)

    def valid(row):
        below = jnp.logical_and(row < 0, first)
        above = jnp.logical_and(row >= BAND, last)
        return jnp.logical_not(jnp.logical_or(below, above))

    def at(i):
        return pl.ds(pl.multiple_of(i * step, step), step)

    def grp(i):
        return pl.ds(pl.multiple_of(i * 32, 32), 32)

    @pl.loop(0, chunks)
    def _(i):
        pre1[:, at(i)] = jnp.dot(w1[...], f3[:, at(i)], preferred_element_type=F32).astype(pre1.dtype)

    @pl.loop(0, 14)
    def _(r):
        act, slope = silu_pair(pre1[grp(r), :].astype(F32))
        act = jnp.where(valid(r - 3), act, 0.0)
        pre1[grp(r), :] = slope.astype(pre1.dtype)
        put_shifted(x3, grp(r), act.astype(BF16), -1)
        x3[grp(r + 14), :] = act.astype(BF16)
        put_shifted(x3, grp(r + 28), act.astype(BF16), 1)

    @pl.loop(0, chunks)
    def _(i):
        for g in (0, 192):
            total = jnp.dot(wmb[:, 0:256], x3[g : g + 256, at(i)], preferred_element_type=F32)
            total = total + jnp.dot(wmb[:, 256:512], x3[448 + g : 704 + g, at(i)], preferred_element_type=F32)
            total = total + jnp.dot(wmb[:, 512:768], x3[896 + g : 1152 + g, at(i)], preferred_element_type=F32)
            pm[g : g + 192, at(i)] = total.astype(pm.dtype)

    @pl.loop(0, 12)
    def _(r):
        act, slope = silu_pair(pm[grp(r), :].astype(F32))
        act = jnp.where(valid(r - 2), act, 0.0)
        slope = jnp.where(valid(r - 2), slope, 0.0)
        pm[grp(r), :] = slope.astype(pm.dtype)
        mid[grp(r), :] = act.astype(BF16)

    gl_acc[...] = jnp.zeros_like(gl_acc)

    @pl.loop(0, chunks)
    def _(i):
        part = mid[32:352, at(i)]
        d24[:, at(i)] = jnp.dot(wl3[...], part, preferred_element_type=F32)
        gl_acc[...] += nt_dot(c3[:, at(i)], part)
        back = pm[:, at(i)].astype(F32) * jnp.dot(wlt[...], c3[:, at(i)], preferred_element_type=F32)
        pm[:, at(i)] = back.astype(pm.dtype)

    den_ref[...] = ds_ref[0:8, :] + d24[8:16, :] + shifted(d24[0:8, :], -1) + shifted(d24[16:24, :], 1)

    @pl.loop(0, 12)
    def _(r):
        back = pm[grp(r), :].astype(F32)
        put_shifted(x3, grp(r), back.astype(BF16), 1)
        mid[grp(r), :] = back.astype(BF16)
        put_shifted(x3, grp(r + 28), back.astype(BF16), -1)

    gf_acc[...] = jnp.zeros_like(gf_acc)
    row = iota((160, step), 0)

    @pl.loop(0, chunks)
    def _(i):
        for g in (0, 160):
            total = jnp.dot(wmtb[:, 0:224], x3[g : g + 224, at(i)], preferred_element_type=F32)
            total = total + jnp.dot(wmtb[:, 256:480], mid[g : g + 224, at(i)], preferred_element_type=F32)
            total = total + jnp.dot(wmtb[:, 512:736], x3[896 + g : 1120 + g, at(i)], preferred_element_type=F32)
            total = total * pre1[64 + g : 224 + g, at(i)].astype(F32)
            gone = jnp.logical_and(row < 32, first) if g == 0 else jnp.logical_and(row >= 128, last)
            bfr[g : g + 160, :] = jnp.where(gone, 0.0, total).astype(BF16)
        back = bfr[...]
        d24[:, at(i)] = jnp.dot(wf3[...], back, preferred_element_type=F32)
        gf_acc[...] += nt_dot(f3[:, at(i)], bfr[32:288, :])

    ge_ref[...] = cot_ref[0:8, :] + d24[8:16, :] + shifted(d24[0:8, :], 1) + shifted(d24[16:24, :], -1)
    blurred = row_blur(ge_ref[...], tab)
    for j in range(n):
        send3[j] = blurred[:, j * BLK : j * BLK + BLK]
    copies3 = exchange(2, lambda to: send3.at[to], cols3)
    cols3[me] = send3[me]

    gm_acc[...] = jnp.zeros_like(gm_acc)

    @pl.loop(0, chunks)
    def _(i):
        act = x3[448 + 64 : 448 + 384, at(i)]
        gm_acc[0] += nt_dot(x3[64:320, at(i)], act)
        gm_acc[1] += nt_dot(mid[64:320, at(i)], act)
        gm_acc[2] += nt_dot(x3[896 + 64 : 896 + 320, at(i)], act)

    share[...] = jnp.zeros_like(share)
    for a in range(3):
        for b in range(3):
            total = gm_acc[b, 0:32, a * 32 : a * 32 + 32]
            for r in range(1, 8):
                total = total + gm_acc[b, r * 32 : r * 32 + 32, (r + a) * 32 : (r + a) * 32 + 32]
            slot = a * 3 + b
            share[slot // 4 * 32 : slot // 4 * 32 + 32, slot % 4 * 32 : slot % 4 * 32 + 32] = total * scale
            total_first = jnp.zeros((1, 32), F32)
            total_last = jnp.zeros((1, 32), F32)
            for r in range(8):
                col = b * 16 + EXT_ROWS.index(r + a - 1)
                total_first = total_first + gf_acc[col : col + 1, r * 32 : r * 32 + 32]
                total_last = total_last + gl_acc[b * 16 + r : b * 16 + r + 1, (r + a) * 32 : (r + a) * 32 + 32]
            share[64 + slot : 65 + slot, 32:64] = total_first * scale
            share[64 + slot : 65 + slot, 64:96] = total_last * scale

    def eight(i):
        return pl.ds(pl.multiple_of(i * 8, 8), 8)

    copies5 = exchange(4, lambda to: share.at[eight(to)], share_in)
    share_in[me] = share[eight(me), :]
    arrive(copies3)
    column_pass(n, width, cols3, padded, adj, tab, None)
    for i in range(n):
        send4[i] = adj[16 + i * 8 : 24 + i * 8, :]
    copies4 = exchange(3, lambda to: send4.at[to], back4)
    back4[me] = send4[me]
    arrive(copies5)
    total = share_in[0]
    for i in range(1, n):
        total = total + share_in[i]
    whole[me] = total
    copies6 = exchange(5, lambda to: whole.at[me], whole)
    arrive(copies4)
    ge_ref[...] = ge_ref[...] - STEP_SIZE * row_blur_adjoint(back4, 8, n, width, tab)
    arrive(copies6)
    for slot in range(9):
        for q in range(4):
            gm_ref[slot, q * 8 : q * 8 + 8, :] = whole[slot // 4 * 4 + q, :, slot % 4 * 32 : slot % 4 * 32 + 32]
        gf_ref[slot] = whole[8 + slot // 8, slot % 8 : slot % 8 + 1, 32:64]
        gl_ref[slot] = whole[8 + slot // 8, slot % 8 : slot % 8 + 1, 64:96]
    for copy in started + near:
        copy.wait_send()


def on_device(n, estimate, observed, cotangent, zone_map, bank_pick, psf_bank, w_first, w_mid, w_last):
    width = estimate.shape[1]
    height = BAND * n
    scale = GRAD_FACTOR / math.sqrt(height * width)
    keep = F32 if width <= 4096 else BF16
    step = 512 if width % 512 == 0 else BLK
    table = width + BLK + height
    vmem, smem = pl.BlockSpec(memory_space=pltpu.VMEM), pl.BlockSpec(memory_space=pltpu.SMEM)
    block = pltpu.VMEM((n, 8, BLK), F32)
    tall = pltpu.VMEM((n, 16, BLK), F32)
    ends = jnp.stack([
        jnp.transpose(w_first, (2, 3, 1, 0)).reshape(9, CH), jnp.transpose(w_last, (2, 3, 0, 1)).reshape(9, CH)])
    middle = jnp.transpose(w_mid, (2, 3, 0, 1)).reshape(9, CH, CH)
    denoised, grad_estimate, grad_mid, grad_first, grad_last = pl.pallas_call(
        functools.partial(kernel, n, scale),
        out_shape=(
            jax.ShapeDtypeStruct((8, width), F32),
            jax.ShapeDtypeStruct((8, width), F32),
            jax.ShapeDtypeStruct((9, CH, CH), F32),
            jax.ShapeDtypeStruct((9, 1, CH), F32),
            jax.ShapeDtypeStruct((9, 1, CH), F32),
        ),
        in_specs=[vmem, vmem, vmem, smem, smem, vmem, vmem, vmem],
        out_specs=[vmem] * 5,
        scratch_shapes=[
            pltpu.VMEM((32, table), F32),
            pltpu.VMEM((8, table), F32),
            block, block, tall, tall, block, block, block, block,
            pltpu.VMEM((8 * n, BLK), F32), block, block,
            pltpu.VMEM((max(height, BLK) + 64, BLK), F32),
            pltpu.VMEM((height + 32, BLK), F32),
            pltpu.VMEM((2, 8, width), F32),
            pltpu.VMEM((2, 8, width), F32),
            pltpu.VMEM((16, width), F32),
            pltpu.VMEM((16, width), F32),
            pltpu.VMEM((448, 48), BF16),
            pltpu.VMEM((384, 48), BF16),
            pltpu.VMEM((24, 320), BF16),
            pltpu.VMEM((24, 320), BF16),
            pltpu.VMEM((192, 768), BF16),
            pltpu.VMEM((160, 768), BF16),
            pltpu.VMEM((48, width), BF16),
            pltpu.VMEM((48, width), BF16),
            pltpu.VMEM((448, width), keep),
            pltpu.VMEM((1344, width), BF16),
            pltpu.VMEM((384, width), keep),
            pltpu.VMEM((384, width), BF16),
            pltpu.VMEM((320, step), BF16),
            pltpu.VMEM((24, width), F32),
            pltpu.VMEM((3, 256, 320), F32),
            pltpu.VMEM((48, 256), F32),
            pltpu.VMEM((48, 320), F32),
            pltpu.SemaphoreType.DMA((6, n - 1)),
            pltpu.SemaphoreType.DMA((6, n - 1)),
            pltpu.SemaphoreType.DMA((2,)),
            pltpu.SemaphoreType.DMA((2,)),
        ],
        compiler_params=pltpu.CompilerParams(
            collective_id=0, has_side_effects=True, vmem_limit_bytes=56 << 20 if width <= 4096 else 64 << 20),
    )(estimate, observed, cotangent, zone_map, bank_pick, psf_bank,
      ends, middle)
    grad_mid = jnp.transpose(grad_mid.reshape(3, 3, CH, CH), (2, 3, 0, 1))
    grad_first = jnp.transpose(grad_first.reshape(3, 3, 1, CH), (3, 2, 0, 1))
    grad_last = jnp.transpose(grad_last.reshape(3, 3, 1, CH), (2, 3, 0, 1))
    return denoised, grad_estimate, grad_first, grad_mid, grad_last


def solution(mesh):
    placed = (
        P(("parts", "rows"), None),
        P("parts", "rows"),
        P(("parts", "rows"), None),
        P("parts", None),
        P(), P(), P(), P(), P(),
    )
    return jax.shard_map(
        functools.partial(on_device, mesh.shape["rows"]),
        mesh=mesh,
        in_specs=placed,
        out_specs=(
            P(("parts", "rows"), None),
            P(("parts", "rows"), None),
            P("parts", None, None, None),
            P("parts", None, None, None),
            P("parts", None, None, None),
        ),
        check_vma=False,
    )
```

```python
import functools
import math

import jax
import jax.numpy as jnp
from jax import lax
from jax.experimental import pallas as pl
from jax.experimental.pallas import tpu as pltpu
from jax.sharding import PartitionSpec as P

BLK = 128
RAD = 12
TAPS = 2 * RAD + 1
CH = 32
BAND = 8
STEP_SIZE = 2.0
GRAD_FACTOR = 8.0
MESH = pl.DeviceIdType.MESH
F32 = jnp.float32
BF16 = jnp.bfloat16

EXT_ROWS = list(range(8)) + [-4, -3, -2, -1, 8, 9, 10, 11]


ROWS_14 = list(range(-3, 11))
ROWS_12 = list(range(-2, 10))
ROWS_10 = list(range(-1, 9))
ROWS_8 = list(range(8))


def silu_pair(v):
    s = 0.5 * jnp.tanh(0.5 * v) + 0.5
    return v * s, s * (1.0 + v * (1.0 - s))


def shifted(v, delta):
    width = v.shape[1]
    lane = lax.broadcasted_iota(jnp.int32, v.shape, 1)
    if delta == 1:
        return jnp.where(lane < width - 1, pltpu.roll(v, width - 1, 1), 0.0)
    return jnp.where(lane > 0, pltpu.roll(v, 1, 1), 0.0)


def put_shifted(ref, rows, v, delta):
    width = v.shape[1]
    edge = width - 1 if delta == 1 else 0
    ref[rows, :] = pltpu.roll(v, width - 1 if delta == 1 else 1, 1).astype(BF16)
    ref[rows, edge : edge + 1] = jnp.zeros((v.shape[0], 1), BF16)


def tn_dot(a, b):
    return lax.dot_general(a, b, (((0,), (0,)), ((), ())), preferred_element_type=F32)


def nt_dot(a, b):
    return lax.dot_general(a, b, (((1,), (1,)), ((), ())), preferred_element_type=F32)


def iota(shape, dim):
    return lax.broadcasted_iota(jnp.int32, shape, dim)


def third(v, size):
    return (v >= size).astype(jnp.int32) + (v >= 2 * size).astype(jnp.int32)


def ones_where(cond):
    return jnp.where(cond, 1.0, 0.0).astype(BF16)


def build_table(n, tab, zone_ref, pick_ref, psf_ref, hot, blocks_row, blocks_col):
    me = lax.axis_index("rows")
    row = iota((8, BLK), 0)
    for i in range(blocks_row):
        k = pick_ref[0, zone_ref[me * BAND // BLK, i]]
        hot[:, i * BLK : i * BLK + BLK] = jnp.where(row == k, 1.0, 0.0)
    hot[:, blocks_row * BLK : blocks_row * BLK + BLK] = jnp.zeros((8, BLK), F32)
    for i in range(blocks_col):
        k = pick_ref[1, zone_ref[i, me]]
        at = (blocks_row + 1 + i) * BLK
        hot[:, at : at + BLK] = jnp.where(row == k, 1.0, 0.0)
    psf = psf_ref[...]
    norm = psf / jnp.sum(psf, axis=1, keepdims=True)
    tab[0:TAPS, :] = lax.dot_general(
        norm, hot[...], (((0,), (0,)), ((), ())), preferred_element_type=F32, precision=lax.Precision.HIGHEST)


def build_weights(wfl_ref, w9_ref, w1, wlt, wl3, wf3, wmb, wmtb):
    wf, wl = wfl_ref[0], wfl_ref[1]
    k, lane = iota((9, 48), 0), iota((9, 48), 1)
    ka = third(k, 3)
    kb = k - 3 * ka
    lb = third(lane, 16)
    le = lane - 16 * lb
    same = kb == lb

    def select(row, sign):
        hit = None
        for a in range(3):
            q = row + sign * (a - 1)
            if q in EXT_ROWS:
                here = jnp.logical_and(ka == a, le == EXT_ROWS.index(q))
                hit = here if hit is None else jnp.logical_or(hit, here)
        return ones_where(jnp.logical_and(same, hit))

    for i, r in enumerate(ROWS_14):
        w1[i * 32 : i * 32 + 32, :] = tn_dot(wf, select(r, 1)).astype(BF16)
    for i, r in enumerate(ROWS_12):
        wlt[i * 32 : i * 32 + 32, :] = tn_dot(wl, select(r, -1)).astype(BF16)
    out, k = iota((24, 9), 0), iota((24, 9), 1)
    ob = third(out, 8)
    orow = out - 8 * ob
    ka = third(k, 3)
    same = k - 3 * ka == ob
    for i, q in enumerate(ROWS_10):
        fwd = ones_where(jnp.logical_and(same, ka == q - orow + 1))
        wl3[:, i * 32 : i * 32 + 32] = jnp.dot(fwd, wl, preferred_element_type=F32).astype(BF16)
        adj = ones_where(jnp.logical_and(same, ka == orow - q + 1))
        wf3[:, i * 32 : i * 32 + 32] = jnp.dot(adj, wf, preferred_element_type=F32).astype(BF16)
    eye = ones_where(iota((32, 32), 0) == iota((32, 32), 1))
    wmb[...] = jnp.zeros_like(wmb)
    wmtb[...] = jnp.zeros_like(wmtb)
    for b in range(3):
        line = jnp.concatenate([w9_ref[a * 3 + b] for a in range(3)], axis=1)
        for r in range(6):
            wmb[r * 32 : r * 32 + 32, b * 256 + r * 32 : b * 256 + r * 32 + 96] = line
        turned = [nt_dot(eye, w9_ref[(2 - a) * 3 + b]) for a in range(3)]
        turned = jnp.concatenate(turned, axis=1).astype(BF16)
        for r in range(5):
            wmtb[r * 32 : r * 32 + 32, b * 256 + r * 32 : b * 256 + r * 32 + 96] = turned


def row_blur(values, tab):
    width = values.shape[1]
    wide = jnp.concatenate([values, jnp.zeros((BAND, BLK), F32)], axis=1)
    blurred = jnp.zeros((BAND, width), F32)
    for t in range(TAPS):
        moved = wide if t == RAD else pltpu.roll(wide, (RAD - t) % (width + BLK), 1)
        blurred = blurred + tab[t : t + 1, 0:width] * moved[:, 0:width]
    return blurred


def row_blur_adjoint(back, rows, n, width, tab):
    end = width + BLK
    wide = jnp.concatenate([back[j].astype(F32) for j in range(n)] + [jnp.zeros((rows, BLK), F32)], axis=1)
    total = jnp.zeros((rows, end), F32)
    for t in range(TAPS):
        part = tab[t : t + 1, 0:end] * wide
        total = total + (part if t == RAD else pltpu.roll(part, (t - RAD) % end, 1))
    return total[:, 0:width]


def column_pass(n, width, cols, padded, adj, tab, target):
    height = BAND * n
    blocks = height // BLK
    padded[...] = jnp.zeros_like(padded)
    for i in range(n):
        padded[16 + i * 8 : 24 + i * 8, :] = cols[i].astype(F32)
    results = []
    for blk in range(blocks):
        lanes = slice(width + (blk + 1) * BLK, width + (blk + 2) * BLK)
        total = jnp.zeros((BLK, BLK), F32)
        for t in range(TAPS):
            start = 16 + blk * BLK + t - RAD
            total = total + tab[t : t + 1, lanes] * padded[start : start + BLK, :]
        if target is not None:
            total = total - target[blk * BLK : blk * BLK + BLK, :]
        results.append(total)
    padded[...] = jnp.zeros_like(padded)
    adj[...] = jnp.zeros_like(adj)
    for blk in range(blocks):
        lanes = slice(width + (blk + 1) * BLK, width + (blk + 2) * BLK)
        padded[32 : 32 + BLK, :] = results[blk]
        total = jnp.zeros((BLK + 32, BLK), F32)
        for t in range(TAPS):
            start = 16 - t + RAD
            total = total + tab[t : t + 1, lanes] * padded[start : start + BLK + 32, :]
        adj[blk * BLK : blk * BLK + BLK + 32, :] = adj[blk * BLK : blk * BLK + BLK + 32, :] + total
    adj[0:16, :] = jnp.zeros((16, BLK), F32)
    adj[16 + height : 32 + height, :] = jnp.zeros((16, BLK), F32)


def kernel(
    n, scale,
    est_ref, obs_ref, cot_in_ref, zone_ref, pick_ref, psf_ref, wfl_ref, w9_ref,
    den_ref, ge_ref, gm_ref, gf_ref, gl_ref,
    tab, hot, send1, cols1, send2, back2, send3, cols3, send4, back4, share, share_in, whole, padded, adj,
    hx_send, hx_recv, ds_ref, cot_ref,
    w1, wlt, wl3, wf3, wmb, wmtb, f3, c3, pre1, x3, pm, mid, bfr, d24, gm_acc, gf_acc, gl_acc,
    send_sems, recv_sems, hs, hr,
):
    me = lax.axis_index("rows")
    width = est_ref.shape[1]
    step = bfr.shape[1]
    chunks = width // step
    first, last = me == 0, me == n - 1
    started = []

    def peer(k):
        return lax.rem(me + k, n)

    barrier = pltpu.get_barrier_semaphore()
    for k in range(1, n):
        pl.semaphore_signal(barrier, inc=1, device_id={"rows": peer(k)}, device_id_type=MESH)

    def exchange(index, src_at, dst):
        copies = []
        for k in range(1, n):
            to = peer(k)
            copies.append(pltpu.make_async_remote_copy(
                src_ref=src_at(to), dst_ref=dst.at[me],
                send_sem=send_sems.at[index, k - 1], recv_sem=recv_sems.at[index, k - 1],
                device_id={"rows": to}, device_id_type=MESH))
        for copy in copies:
            copy.start()
        started.extend(copies)
        return copies

    def arrive(copies):
        for copy in copies:
            copy.wait_recv()

    build_table(n, tab, zone_ref, pick_ref, psf_ref, hot, width // BLK, BAND * n // BLK)
    blurred = row_blur(est_ref[...], tab)
    for j in range(n):
        send1[j] = blurred[:, j * BLK : j * BLK + BLK].astype(BF16)
    hx_send[0, 0:4, :] = est_ref[4:8, :]
    hx_send[0, 4:8, :] = cot_in_ref[4:8, :]
    hx_send[1, 0:4, :] = est_ref[0:4, :]
    hx_send[1, 4:8, :] = cot_in_ref[0:4, :]
    pl.semaphore_wait(barrier, n - 1)
    copies1 = exchange(0, lambda to: send1.at[to], cols1)
    near = []
    for side, k in ((0, 1), (1, n - 1)):
        near.append(pltpu.make_async_remote_copy(
            src_ref=hx_send.at[side], dst_ref=hx_recv.at[side], send_sem=hs.at[side], recv_sem=hr.at[side],
            device_id={"rows": peer(k)}, device_id_type=MESH))
    for copy in near:
        copy.start()
    cols1[me] = send1[me]
    build_weights(wfl_ref, w9_ref, w1, wlt, wl3, wf3, wmb, wmtb)
    arrive(copies1)
    column_pass(n, width, cols1, padded, adj, tab, obs_ref)
    sub = iota((BAND, BLK), 0)
    for i in range(n):
        base = 16 + i * 8
        halo = jnp.where(sub < 4, adj[base - 4 : base + 4, :], adj[base + 4 : base + 12, :])
        send2[i] = jnp.concatenate([adj[base : base + 8, :], halo], axis=0).astype(BF16)
    copies2 = exchange(1, lambda to: send2.at[to], back2)
    back2[me] = send2[me]

    sub = iota((16, width), 0)
    outside = jnp.logical_or(
        jnp.logical_and(jnp.logical_and(sub >= 8, sub < 12), first), jnp.logical_and(sub >= 12, last))
    arrive(near)
    cot_ref[0:8, :] = cot_in_ref[...]
    cot_ref[8:12, :] = hx_recv[0, 4:8, :]
    cot_ref[12:16, :] = hx_recv[1, 4:8, :]
    ds_ref[0:8, :] = est_ref[...]
    ds_ref[8:12, :] = hx_recv[0, 0:4, :]
    ds_ref[12:16, :] = hx_recv[1, 0:4, :]
    cot = jnp.where(outside, 0.0, cot_ref[...])
    c3[0:16, :] = shifted(cot, 1).astype(BF16)
    c3[16:32, :] = cot.astype(BF16)
    c3[32:48, :] = shifted(cot, -1).astype(BF16)
    arrive(copies2)

    ds = ds_ref[...] - STEP_SIZE * row_blur_adjoint(back2, 16, n, width, tab)
    ds = jnp.where(outside, 0.0, ds)
    ds_ref[...] = ds
    f3[0:16, :] = shifted(ds, -1).astype(BF16)
    f3[16:32, :] = ds.astype(BF16)
    f3[32:48, :] = shifted(ds, 1).astype(BF16)

    def valid(row):
        below = jnp.logical_and(row < 0, first)
        above = jnp.logical_and(row >= BAND, last)
        return jnp.logical_not(jnp.logical_or(below, above))

    def at(i):
        return pl.ds(pl.multiple_of(i * step, step), step)

    def grp(i):
        return pl.ds(pl.multiple_of(i * 32, 32), 32)

    @pl.loop(0, chunks)
    def _(i):
        pre1[:, at(i)] = jnp.dot(w1[...], f3[:, at(i)], preferred_element_type=F32).astype(pre1.dtype)

    @pl.loop(0, 14)
    def _(r):
        act, slope = silu_pair(pre1[grp(r), :].astype(F32))
        act = jnp.where(valid(r - 3), act, 0.0)
        pre1[grp(r), :] = slope.astype(pre1.dtype)
        put_shifted(x3, grp(r), act.astype(BF16), -1)
        x3[grp(r + 14), :] = act.astype(BF16)
        put_shifted(x3, grp(r + 28), act.astype(BF16), 1)

    @pl.loop(0, chunks)
    def _(i):
        for g in (0, 192):
            total = jnp.dot(wmb[:, 0:256], x3[g : g + 256, at(i)], preferred_element_type=F32)
            total = total + jnp.dot(wmb[:, 256:512], x3[448 + g : 704 + g, at(i)], preferred_element_type=F32)
            total = total + jnp.dot(wmb[:, 512:768], x3[896 + g : 1152 + g, at(i)], preferred_element_type=F32)
            pm[g : g + 192, at(i)] = total.astype(pm.dtype)

    @pl.loop(0, 12)
    def _(r):
        act, slope = silu_pair(pm[grp(r), :].astype(F32))
        act = jnp.where(valid(r - 2), act, 0.0)
        slope = jnp.where(valid(r - 2), slope, 0.0)
        pm[grp(r), :] = slope.astype(pm.dtype)
        mid[grp(r), :] = act.astype(BF16)

    gl_acc[...] = jnp.zeros_like(gl_acc)

    @pl.loop(0, chunks)
    def _(i):
        part = mid[32:352, at(i)]
        d24[:, at(i)] = jnp.dot(wl3[...], part, preferred_element_type=F32)
        gl_acc[...] += nt_dot(c3[:, at(i)], part)
        back = pm[:, at(i)].astype(F32) * jnp.dot(wlt[...], c3[:, at(i)], preferred_element_type=F32)
        pm[:, at(i)] = back.astype(pm.dtype)

    den_ref[...] = ds_ref[0:8, :] + d24[8:16, :] + shifted(d24[0:8, :], -1) + shifted(d24[16:24, :], 1)

    @pl.loop(0, 12)
    def _(r):
        back = pm[grp(r), :].astype(F32)
        put_shifted(x3, grp(r), back.astype(BF16), 1)
        mid[grp(r), :] = back.astype(BF16)
        put_shifted(x3, grp(r + 28), back.astype(BF16), -1)

    gf_acc[...] = jnp.zeros_like(gf_acc)
    row = iota((160, step), 0)

    @pl.loop(0, chunks)
    def _(i):
        for g in (0, 160):
            total = jnp.dot(wmtb[:, 0:224], x3[g : g + 224, at(i)], preferred_element_type=F32)
            total = total + jnp.dot(wmtb[:, 256:480], mid[g : g + 224, at(i)], preferred_element_type=F32)
            total = total + jnp.dot(wmtb[:, 512:736], x3[896 + g : 1120 + g, at(i)], preferred_element_type=F32)
            total = total * pre1[64 + g : 224 + g, at(i)].astype(F32)
            gone = jnp.logical_and(row < 32, first) if g == 0 else jnp.logical_and(row >= 128, last)
            bfr[g : g + 160, :] = jnp.where(gone, 0.0, total).astype(BF16)
        back = bfr[...]
        d24[:, at(i)] = jnp.dot(wf3[...], back, preferred_element_type=F32)
        gf_acc[...] += nt_dot(f3[:, at(i)], bfr[32:288, :])

    ge_ref[...] = cot_ref[0:8, :] + d24[8:16, :] + shifted(d24[0:8, :], 1) + shifted(d24[16:24, :], -1)
    blurred = row_blur(ge_ref[...], tab)
    for j in range(n):
        send3[j] = blurred[:, j * BLK : j * BLK + BLK].astype(BF16)
    copies3 = exchange(2, lambda to: send3.at[to], cols3)
    cols3[me] = send3[me]

    gm_acc[...] = jnp.zeros_like(gm_acc)

    @pl.loop(0, chunks)
    def _(i):
        act = x3[448 + 64 : 448 + 384, at(i)]
        gm_acc[0] += nt_dot(x3[64:320, at(i)], act)
        gm_acc[1] += nt_dot(mid[64:320, at(i)], act)
        gm_acc[2] += nt_dot(x3[896 + 64 : 896 + 320, at(i)], act)

    share[...] = jnp.zeros_like(share)
    for a in range(3):
        for b in range(3):
            total = gm_acc[b, 0:32, a * 32 : a * 32 + 32]
            for r in range(1, 8):
                total = total + gm_acc[b, r * 32 : r * 32 + 32, (r + a) * 32 : (r + a) * 32 + 32]
            slot = a * 3 + b
            share[slot // 4 * 32 : slot // 4 * 32 + 32, slot % 4 * 32 : slot % 4 * 32 + 32] = total * scale
            total_first = jnp.zeros((1, 32), F32)
            total_last = jnp.zeros((1, 32), F32)
            for r in range(8):
                col = b * 16 + EXT_ROWS.index(r + a - 1)
                total_first = total_first + gf_acc[col : col + 1, r * 32 : r * 32 + 32]
                total_last = total_last + gl_acc[b * 16 + r : b * 16 + r + 1, (r + a) * 32 : (r + a) * 32 + 32]
            share[64 + slot : 65 + slot, 32:64] = total_first * scale
            share[64 + slot : 65 + slot, 64:96] = total_last * scale

    def eight(i):
        return pl.ds(pl.multiple_of(i * 8, 8), 8)

    copies5 = exchange(4, lambda to: share.at[eight(to)], share_in)
    share_in[me] = share[eight(me), :]
    arrive(copies3)
    column_pass(n, width, cols3, padded, adj, tab, None)
    for i in range(n):
        send4[i] = adj[16 + i * 8 : 24 + i * 8, :].astype(BF16)
    copies4 = exchange(3, lambda to: send4.at[to], back4)
    back4[me] = send4[me]
    arrive(copies5)
    total = share_in[0]
    for i in range(1, n):
        total = total + share_in[i]
    whole[me] = total
    copies6 = exchange(5, lambda to: whole.at[me], whole)
    arrive(copies4)
    ge_ref[...] = ge_ref[...] - STEP_SIZE * row_blur_adjoint(back4, 8, n, width, tab)
    arrive(copies6)
    for slot in range(9):
        for q in range(4):
            gm_ref[slot, q * 8 : q * 8 + 8, :] = whole[slot // 4 * 4 + q, :, slot % 4 * 32 : slot % 4 * 32 + 32]
        gf_ref[slot] = whole[8 + slot // 8, slot % 8 : slot % 8 + 1, 32:64]
        gl_ref[slot] = whole[8 + slot // 8, slot % 8 : slot % 8 + 1, 64:96]
    for copy in started + near:
        copy.wait_send()


def on_device(n, estimate, observed, cotangent, zone_map, bank_pick, psf_bank, w_first, w_mid, w_last):
    width = estimate.shape[1]
    height = BAND * n
    scale = GRAD_FACTOR / math.sqrt(height * width)
    keep = F32 if width <= 4096 else BF16
    step = 512 if width % 512 == 0 else BLK
    table = width + BLK + height
    vmem, smem = pl.BlockSpec(memory_space=pltpu.VMEM), pl.BlockSpec(memory_space=pltpu.SMEM)
    block = pltpu.VMEM((n, 8, BLK), F32)
    flat = pltpu.VMEM((n, 8, BLK), BF16)
    tall = pltpu.VMEM((n, 16, BLK), BF16)
    ends = jnp.stack([
        jnp.transpose(w_first, (2, 3, 1, 0)).reshape(9, CH), jnp.transpose(w_last, (2, 3, 0, 1)).reshape(9, CH)])
    middle = jnp.transpose(w_mid, (2, 3, 0, 1)).reshape(9, CH, CH)
    denoised, grad_estimate, grad_mid, grad_first, grad_last = pl.pallas_call(
        functools.partial(kernel, n, scale),
        out_shape=(
            jax.ShapeDtypeStruct((8, width), F32),
            jax.ShapeDtypeStruct((8, width), F32),
            jax.ShapeDtypeStruct((9, CH, CH), F32),
            jax.ShapeDtypeStruct((9, 1, CH), F32),
            jax.ShapeDtypeStruct((9, 1, CH), F32),
        ),
        in_specs=[vmem, vmem, vmem, smem, smem, vmem, vmem, vmem],
        out_specs=[vmem] * 5,
        scratch_shapes=[
            pltpu.VMEM((32, table), F32),
            pltpu.VMEM((8, table), F32),
            flat, flat, tall, tall, flat, flat, flat, flat,
            pltpu.VMEM((8 * n, BLK), F32), block, block,
            pltpu.VMEM((max(height, BLK) + 64, BLK), F32),
            pltpu.VMEM((height + 32, BLK), F32),
            pltpu.VMEM((2, 8, width), F32),
            pltpu.VMEM((2, 8, width), F32),
            pltpu.VMEM((16, width), F32),
            pltpu.VMEM((16, width), F32),
            pltpu.VMEM((448, 48), BF16),
            pltpu.VMEM((384, 48), BF16),
            pltpu.VMEM((24, 320), BF16),
            pltpu.VMEM((24, 320), BF16),
            pltpu.VMEM((192, 768), BF16),
            pltpu.VMEM((160, 768), BF16),
            pltpu.VMEM((48, width), BF16),
            pltpu.VMEM((48, width), BF16),
            pltpu.VMEM((448, width), keep),
            pltpu.VMEM((1344, width), BF16),
            pltpu.VMEM((384, width), keep),
            pltpu.VMEM((384, width), BF16),
            pltpu.VMEM((320, step), BF16),
            pltpu.VMEM((24, width), F32),
            pltpu.VMEM((3, 256, 320), F32),
            pltpu.VMEM((48, 256), F32),
            pltpu.VMEM((48, 320), F32),
            pltpu.SemaphoreType.DMA((6, n - 1)),
            pltpu.SemaphoreType.DMA((6, n - 1)),
            pltpu.SemaphoreType.DMA((2,)),
            pltpu.SemaphoreType.DMA((2,)),
        ],
        compiler_params=pltpu.CompilerParams(
            collective_id=0, has_side_effects=True, vmem_limit_bytes=56 << 20 if width <= 4096 else 64 << 20),
    )(estimate, observed, cotangent, zone_map, bank_pick, psf_bank,
      ends, middle)
    grad_mid = jnp.transpose(grad_mid.reshape(3, 3, CH, CH), (2, 3, 0, 1))
    grad_first = jnp.transpose(grad_first.reshape(3, 3, 1, CH), (3, 2, 0, 1))
    grad_last = jnp.transpose(grad_last.reshape(3, 3, 1, CH), (2, 3, 0, 1))
    return denoised, grad_estimate, grad_first, grad_mid, grad_last


def solution(mesh):
    placed = (
        P(("parts", "rows"), None),
        P("parts", "rows"),
        P(("parts", "rows"), None),
        P("parts", None),
        P(), P(), P(), P(), P(),
    )
    return jax.shard_map(
        functools.partial(on_device, mesh.shape["rows"]),
        mesh=mesh,
        in_specs=placed,
        out_specs=(
            P(("parts", "rows"), None),
            P(("parts", "rows"), None),
            P("parts", None, None, None),
            P("parts", None, None, None),
            P("parts", None, None, None),
        ),
        check_vma=False,
    )
```
